256 devices in a mesh: blk: 128 (over z, y, x_hi, core), help: 2 (over x_lo).
Axes of the slice: x: 4 (x_hi: 2, x_lo: 2; x = x_hi * 2 + x_lo), y: 4, z: 8, core: 2. Of those that a mesh axis runs over, the one named last changes fastest.
Arguments:
- heads: float32 [32768, 400], P(('blk', 'help')), may hold values from -6 to 6
- tails: float32 [32768, 400], P(('blk', 'help')), may hold values from -6 to 6
- head_acc: float32 [32768], P(('blk', 'help')), may hold values from 0.01 to 0.1
- tail_acc: float32 [32768], P(('blk', 'help')), may hold values from 0.01 to 0.1
- relations: bfloat16 [7424, 400], replicated, may hold values from -0.59765625 to 0.59765625
- counts: int32 [4, 256], P(None, ('blk', 'help')), may hold values from 1 to 5, as said below
- rel_ids: int32 [4, 256, 5], P(None, ('blk', 'help')), may hold values from 0 to 7423
- head_edges: int32 [4, 256, 5, 1024], P(None, ('blk', 'help')), may hold values from 0 to 127
- tail_edges: int32 [4, 256, 5, 1024], P(None, ('blk', 'help')), may hold values from 0 to 127
Outputs:
- new_heads: float32 [32768, 400], P(('blk', 'help'))
- new_tails: float32 [32768, 400], P(('blk', 'help'))
- new_head_acc: float32 [32768], P(('blk', 'help'))
- new_tail_acc: float32 [32768], P(('blk', 'help'))
The draws below stay inside these ranges and needn't reach their ends.
Inputs may be any that keep to these rules, and one draw needn't show every extreme that they name: `counts`: in every round the two partitions 2 q and 2 q + 1 have one count from 3 to 5 and the other 1 or 2; in every round partitions 0 and 1 hold 5 and 1.
All inputs are finite; a program needn't handle non-finite values.
Results may differ from the reference program's by a relative error of at most 0.0003.
Values sent between devices are 32-bit elements; how exact they have to be, the bound alone decides.
No kernel may reach another device: no remote copies, remote signals or barrier semaphores. Data moves between devices by JAX's collectives and lax.ppermute only.
A program may use at most 64 MiB of HBM per device.

```python
import math
from functools import partial
import jax
import jax.numpy as jnp
from jax import lax

D = 400
RELS = 7424
ROWS = 128
EDGES = 1024
MAXT = 5
ROUNDS = 4
PARTITIONS = 256
ENT = 32768
N_BLK = 128
N_HELP = 2


def draw_counts(key, part):
    keys = jax.random.split(jax.random.fold_in(key, 7), 3)
    pair_count = PARTITIONS // 2
    high = jax.random.randint(keys[0], (ROUNDS, pair_count), 3, MAXT + 1)
    low = jax.random.randint(keys[1], (ROUNDS, pair_count), 1, 3)
    high = high.at[:, 0].set(MAXT)
    low = low.at[:, 0].set(1)
    flip = jax.random.randint(keys[2], (ROUNDS, pair_count), 0, 2)
    flip = flip.at[:, 0].set(1)
    first_part = jnp.where(flip == 1, high, low)
    second_part = jnp.where(flip == 1, low, high)
    return jnp.stack([first_part, second_part], axis=-1).reshape(ROUNDS, PARTITIONS).astype(jnp.int32)


def set_ends(entries, key, smallest, largest):
    longest = entries.shape.index(max(entries.shape))
    spots = []
    for shift in (0, 1):
        where = [jax.random.randint(jax.random.fold_in(key, axis), (), 0, length) for axis, length in enumerate(entries.shape)]
        where[longest] = (where[longest] + shift) % entries.shape[longest]
        spots.append(tuple(where))
    return entries.at[spots[0]].set(smallest).at[spots[1]].set(largest)


def block_levels(own_key, dims, cuts, smallest, largest):
    loudness, own = 1.0, jax.random.fold_in(own_key, 6)
    for axis_at, shards_of in cuts:
        draws = jnp.exp(jax.random.uniform(jax.random.fold_in(own, axis_at), (shards_of,), jnp.float32, smallest / len(cuts), largest / len(cuts)))
        loudness = loudness * jnp.repeat(draws, dims[axis_at] // shards_of).reshape([-1 if axis == axis_at else 1 for axis in range(len(dims))])
    return loudness


def bell_draw(stream_key, shape, deviation, limit, cuts=(), kind=jnp.bfloat16):
    values = jax.random.normal(stream_key, shape, jnp.float32) * deviation
    if len(cuts) > 0:
        values = block_levels(stream_key, shape, cuts, -0.22, 0.18) * values
    return jnp.clip(values, min=-limit, max=limit).astype(kind)


def setup_inputs(seed: int = 0) -> dict:
    seeds = jax.random.split(jax.random.key(seed), 10)
    return {
        "heads": bell_draw(seeds[0], (ENT, D), 1.0, 6.0, ((0, 256),), jnp.float32),
        "tails": bell_draw(seeds[1], (ENT, D), 1.0, 6.0, ((0, 256),), jnp.float32),
        "head_acc": jnp.clip(jnp.exp(math.log(0.1) - 2.3025851 * jax.random.uniform(seeds[2], (ENT,), jnp.float32) ** block_levels(seeds[2], (ENT,), ((0, 256),), -0.2, 0.2)), 0.01, 0.1),
        "tail_acc": jnp.clip(jnp.exp(math.log(0.1) - 2.3025851 * jax.random.uniform(seeds[3], (ENT,), jnp.float32) ** block_levels(seeds[3], (ENT,), ((0, 256),), -0.2, 0.2)), 0.01, 0.1),
        "relations": bell_draw(seeds[4], (RELS, D), 0.1, 0.59765625),
        "counts": draw_counts(jax.random.fold_in(seeds[9], 71), 0),
        "rel_ids": set_ends(jax.random.randint(seeds[6], (ROUNDS, PARTITIONS, MAXT), 0, RELS), jax.random.fold_in(seeds[6], 1), 0, RELS - 1).astype(jnp.int32),
        "head_edges": set_ends(jax.random.randint(seeds[7], (ROUNDS, PARTITIONS, MAXT, EDGES), 0, ROWS), jax.random.fold_in(seeds[7], 1), 0, ROWS - 1).astype(jnp.int32),
        "tail_edges": set_ends(jax.random.randint(seeds[8], (ROUNDS, PARTITIONS, MAXT, EDGES), 0, ROWS), jax.random.fold_in(seeds[8], 1), 0, ROWS - 1).astype(jnp.int32),
    }


NEG_WEIGHT = 0.0625
LEARN_RATE = 0.1
HIGH = lax.Precision.HIGHEST

def task_grads(head_block, tail_block, rel_vec, head_index, tail_index):
    row_count = head_block.shape[0]
    scaled = head_block * rel_vec[None, :]
    scores = lax.dot_general(scaled, tail_block, (((1,), (1,)), ((), ())), precision=HIGH, preferred_element_type=jnp.float32)
    labels = jnp.zeros((row_count, row_count), jnp.float32).at[head_index, tail_index].add(1.0)
    coefficient = NEG_WEIGHT * jax.nn.sigmoid(scores) - labels
    head_grad = jnp.dot(coefficient, tail_block, precision=HIGH, preferred_element_type=jnp.float32) * rel_vec[None, :]
    tail_grad = lax.dot_general(coefficient, scaled, (((0,), (0,)), ((), ())), precision=HIGH, preferred_element_type=jnp.float32)
    return (head_grad, tail_grad)

def adagrad(block, state, grad):
    new_state = state + lax.optimization_barrier(jnp.mean(grad * grad, axis=1))
    return (block - LEARN_RATE * grad / jnp.sqrt(new_state)[:, None], new_state)

def bucket(packed, relations):
    head_block, tail_block, head_state, tail_state, task_count, rel_row, head_rows, tail_rows = packed

    def add_task(slot_id, totals):
        rel_vec = relations[rel_row[slot_id]].astype(jnp.float32)
        head_grad, tail_grad = task_grads(head_block, tail_block, rel_vec, head_rows[slot_id], tail_rows[slot_id])
        return (totals[0] + head_grad, totals[1] + tail_grad)
    empty = jnp.zeros(head_block.shape, jnp.float32)
    head_grad, tail_grad = lax.fori_loop(jnp.int32(0), task_count.astype(jnp.int32), add_task, (empty, empty))
    new_head, new_head_state = adagrad(head_block, head_state, head_grad)
    new_tail, new_tail_state = adagrad(tail_block, tail_state, tail_grad)
    return (new_head, new_tail, new_head_state, new_tail_state)

def reference(heads, tails, head_acc, tail_acc, relations, counts, rel_ids, head_edges, tail_edges):
    head_grid = heads.reshape(N_BLK, N_HELP, ROWS, D)
    tail_grid = tails.reshape(N_BLK, N_HELP, ROWS, D)
    head_state = head_acc.reshape(N_BLK, N_HELP, ROWS)
    tail_state = tail_acc.reshape(N_BLK, N_HELP, ROWS)
    for round_ix in range(ROUNDS):
        tail_here = jnp.roll(tail_grid, round_ix, axis=0).reshape(PARTITIONS, ROWS, D)
        state_here = jnp.roll(tail_state, round_ix, axis=0).reshape(PARTITIONS, ROWS)
        outcome = lax.map(partial(bucket, relations=relations), (head_grid.reshape(PARTITIONS, ROWS, D), tail_here, head_state.reshape(PARTITIONS, ROWS), state_here, counts[round_ix], rel_ids[round_ix], head_edges[round_ix], tail_edges[round_ix]))
        head_grid = outcome[0].reshape(N_BLK, N_HELP, ROWS, D)
        tail_grid = jnp.roll(outcome[1].reshape(N_BLK, N_HELP, ROWS, D), -round_ix, axis=0)
        head_state = outcome[2].reshape(N_BLK, N_HELP, ROWS)
        tail_state = jnp.roll(outcome[3].reshape(N_BLK, N_HELP, ROWS), -round_ix, axis=0)
    return (head_grid.reshape(ENT, D), tail_grid.reshape(ENT, D), head_state.reshape(ENT), tail_state.reshape(ENT))
```

```python
import jax
import jax.numpy as jnp
from jax import lax
from jax.experimental import pallas as pl
from jax.experimental.pallas import tpu as pltpu
from jax.sharding import PartitionSpec as P

NEG_WEIGHT = 0.0625
LEARN_RATE = 0.1
F32, BF16 = jnp.float32, jnp.bfloat16
LANES = 128
VMEM = pl.BlockSpec(memory_space=pltpu.VMEM)
SMEM = pl.BlockSpec(memory_space=pltpu.SMEM)
ANY = pl.BlockSpec(memory_space=pl.ANY)


def dot(a, b, dims):
    return lax.dot_general(a, b, (dims, ((), ())), preferred_element_type=F32)


NN, NT, TN = ((1,), (0,)), ((1,), (1,)), ((0,), (0,))


def hi_lo(x):
    hi = x.astype(BF16)
    return hi, (x - hi.astype(F32)).astype(BF16)


def one_hot(rows):
    which = lax.broadcasted_iota(jnp.int32, (LANES, LANES), 0)
    parts = [jnp.where(rows[r : r + 1, :] == which, 1.0, 0.0).astype(BF16) for r in range(8)]
    return jnp.concatenate(parts, axis=1)


def labels(labels_ref, he_ref, te_ref, first, tasks):
    for s in range(tasks):
        labels_ref[s] = dot(one_hot(te_ref[first + s]), one_hot(he_ref[first + s]), NT)


def fetch(rel_ids, rel_ref, rel_buf, sem, first, s):
    start = pl.multiple_of((rel_ids[first + s] // LANES) * LANES, LANES)
    return pltpu.make_async_copy(rel_ref.at[:, pl.ds(start, LANES)], rel_buf.at[s], sem.at[s])


def rel_columns(rel_ids, rel_buf, first, s):
    lane = lax.rem(rel_ids[first + s], LANES)
    pick = (lax.broadcasted_iota(jnp.int32, (LANES, LANES), 0) == lane).astype(F32).astype(BF16)
    return dot(rel_buf[s], pick, NN)


def scale_heads(heads, rel_ids, rel_buf, rel_out, shi, slo, first, tasks):
    for s in range(tasks):
        cols = pl.ds(s * LANES, LANES)
        rel = rel_columns(rel_ids, rel_buf, first, s)
        rel_out[:, cols] = rel.astype(BF16)
        hi, lo = hi_lo(heads * rel)
        shi[:, cols] = hi
        slo[:, cols] = lo


def adagrad(block, state, grad):
    width = block.shape[0]
    state = state + jnp.sum(grad * grad, axis=0, keepdims=True) * (1.0 / width)
    return block - grad * (LEARN_RATE / jnp.sqrt(state)), state


def tail_step(count, tail, state, shi_ref, slo_ref, labels_ref, chi_ref, clo_ref, tasks):
    thi, tlo = hi_lo(tail)
    shi, slo = shi_ref[...], slo_ref[...]
    scores = dot(thi, shi, TN) + dot(tlo, shi, TN) + dot(thi, slo, TN)
    for s in range(tasks):
        cols = pl.ds(s * LANES, LANES)
        score = scores[:, s * LANES : (s + 1) * LANES]
        coefficient = NEG_WEIGHT * (0.5 * jnp.tanh(0.5 * score) + 0.5) - labels_ref[s]
        chi, clo = hi_lo(jnp.where(s < count, coefficient, 0.0))
        chi_ref[:, cols] = chi
        clo_ref[:, cols] = clo
    chi, clo = chi_ref[...], clo_ref[...]
    grad = dot(shi, chi, NT) + dot(slo, chi, NT) + dot(shi, clo, NT)
    return adagrad(tail, state, grad)


def head_step(head, state, tail, rel_ref, chi_ref, clo_ref, tasks):
    thi, tlo = hi_lo(tail)
    grad = None
    for s in range(tasks):
        cols = pl.ds(s * LANES, LANES)
        chi, clo = chi_ref[:, cols], clo_ref[:, cols]
        term = dot(thi, chi, NN) + dot(tlo, chi, NN) + dot(thi, clo, NN)
        term = term * rel_ref[:, cols].astype(F32)
        grad = term if grad is None else grad + term
    return adagrad(head, state, grad)


def put_tail(out_ref, tail, state, width):
    out_ref[pl.ds(0, width), :] = tail
    out_ref[pl.ds(width, 8), :] = jnp.broadcast_to(state, (8, LANES))


def first_kernel(tasks, width):
    def body(counts, rel_ids, head_hbm, tail_hbm, tacc, rel_ref, he_hbm, te_hbm,
             tail_out, chi_ref, clo_ref, rel_out,
             head, tail, he, te, shi, slo, labels_ref, rel_buf, rel_sem, sem):
        edges = [pltpu.make_async_copy(src.at[pl.ds(0, tasks)], dst, sem.at[i])
                 for i, (src, dst) in enumerate(((he_hbm, he), (te_hbm, te)))]
        blocks = [pltpu.make_async_copy(src, dst, sem.at[2 + i])
                  for i, (src, dst) in enumerate(((head_hbm, head), (tail_hbm, tail)))]
        rels = [fetch(rel_ids, rel_ref, rel_buf, rel_sem, 0, s) for s in range(tasks)]
        for copy in edges + rels + blocks:
            copy.start()
        for copy in edges:
            copy.wait()
        labels(labels_ref, he, te, 0, tasks)
        for copy in rels + blocks:
            copy.wait()
        scale_heads(head[...], rel_ids, rel_buf, rel_out, shi, slo, 0, tasks)
        new, state = tail_step(counts[0], tail[...], tacc[...], shi, slo, labels_ref, chi_ref, clo_ref, tasks)
        put_tail(tail_out, new, state, width)

    return body


def tail_kernel(k, tasks, width, last):
    def body(counts, tail_in, shi, slo, labels_ref, *outs):
        tail, state = tail_in[pl.ds(0, width), :], tail_in[pl.ds(width, 1), :]
        chi_ref, clo_ref = outs[-2:]
        new, state = tail_step(counts[k], tail, state, shi, slo, labels_ref, chi_ref, clo_ref, tasks)
        if last:
            outs[0][...] = new
            outs[1][...] = state
        else:
            put_tail(outs[0], new, state, width)

    return body


def head_kernel(k, tasks, width):
    first = (k + 1) * tasks

    def body(rel_ids, head, hacc, tail_in, rel_in, chi_ref, clo_ref, rel_ref, he, te,
             head_out, hacc_out, shi, slo, labels_ref, rel_out, rel_buf, rel_sem):
        rels = [fetch(rel_ids, rel_ref, rel_buf, rel_sem, first, s) for s in range(tasks)]
        for copy in rels:
            copy.start()
        new, state = head_step(head[...], hacc[...], tail_in[pl.ds(0, width), :], rel_in, chi_ref, clo_ref, tasks)
        head_out[...] = new
        hacc_out[...] = state
        labels(labels_ref, he, te, first, tasks)
        for copy in rels:
            copy.wait()
        scale_heads(new, rel_ids, rel_buf, rel_out, shi, slo, first, tasks)

    return body


def last_kernel(tasks, width):
    def body(head, hacc, tail_in, rel_in, chi_ref, clo_ref, head_out, hacc_out):
        new, state = head_step(head[...], hacc[...], tail_in[pl.ds(0, width), :], rel_in, chi_ref, clo_ref, tasks)
        head_out[...] = new
        hacc_out[...] = state

    return body


def call(body, ins, outs, scratch, args, name, flops):
    return pl.pallas_call(
        body,
        in_specs=ins,
        out_specs=[VMEM] * len(outs),
        out_shape=[jax.ShapeDtypeStruct(*o) for o in outs],
        scratch_shapes=scratch,
        compiler_params=pltpu.CompilerParams(vmem_limit_bytes=16 << 20),
        cost_estimate=pl.CostEstimate(flops=flops, bytes_accessed=1 << 20, transcendentals=0),
        name=name,
    )(*args)


def shifted(block, distance):
    n = lax.axis_size("blk")
    return lax.ppermute(block, "blk", [((i - distance) % n, i) for i in range(n)])


def on_device(heads, tails, head_acc, tail_acc, relations, counts, rel_ids, head_edges, tail_edges):
    rounds, _, tasks, edges = head_edges.shape
    rows, width = heads.shape
    head, tail, rels = heads.T, tails.T, relations.T
    hacc, tacc = head_acc.reshape(1, rows), tail_acc.reshape(1, rows)
    counts, rel_ids = counts.reshape(-1), rel_ids.reshape(-1)
    he = head_edges.reshape(rounds * tasks, edges // LANES, LANES)
    te = tail_edges.reshape(rounds * tasks, edges // LANES, LANES)
    wide = tasks * rows
    block, packed, row = ((width, rows), F32), ((width + 8, rows), F32), ((1, rows), F32)
    coeff, scaled, table = ((rows, wide), BF16), ((width, wide), BF16), ((tasks, rows, rows), F32)
    rel_scratch = [pltpu.VMEM((tasks, width, LANES), BF16), pltpu.SemaphoreType.DMA((tasks,))]
    big = 10**9

    sent, chi, clo, rel = call(
        first_kernel(tasks, width),
        [SMEM, SMEM, ANY, ANY, VMEM, ANY, ANY, ANY],
        [packed, coeff, coeff, scaled],
        [pltpu.VMEM(*block), pltpu.VMEM(*block),
         pltpu.VMEM((tasks, edges // LANES, LANES), jnp.int32), pltpu.VMEM((tasks, edges // LANES, LANES), jnp.int32),
         pltpu.VMEM(*scaled), pltpu.VMEM(*scaled), pltpu.VMEM(*table)] + rel_scratch + [pltpu.SemaphoreType.DMA((4,))],
        (counts, rel_ids, head, tail, tacc, rels, he, te), "first", big)
    held = tail
    for k in range(rounds - 1):
        arrived = shifted(sent, 1)
        head, hacc, shi, slo, lab, rel = call(
            head_kernel(k, tasks, width),
            [SMEM, VMEM, VMEM, VMEM, VMEM, VMEM, VMEM, ANY, VMEM, VMEM],
            [block, row, scaled, scaled, table, scaled], rel_scratch,
            (rel_ids, head, hacc, held, rel, chi, clo, rels, he, te), f"heads_{k}", big)
        held = arrived
        last = k == rounds - 2
        *sent, chi, clo = call(
            tail_kernel(k + 1, tasks, width, last),
            [SMEM, VMEM, VMEM, VMEM, VMEM],
            ([block, row] if last else [packed]) + [coeff, coeff], [],
            (counts, held, shi, slo, lab), f"tails_{k + 1}", big)
        sent = tuple(sent) if last else sent[0]
    tail, tacc = shifted(sent, 1 - rounds)
    head, hacc = call(
        last_kernel(tasks, width), [VMEM] * 6, [block, row], [],
        (head, hacc, held, rel, chi, clo), "heads_last", big)
    return head.T, tail.T, hacc.reshape(rows), tacc.reshape(rows)


def solution(mesh):
    split, edge = P(("blk", "help"), None), P(None, ("blk", "help"), None, None)
    flat = P(("blk", "help"))
    return jax.shard_map(
        on_device,
        mesh=mesh,
        in_specs=(split, split, flat, flat, P(), P(None, ("blk", "help")), P(None, ("blk", "help"), None), edge, edge),
        out_specs=(split, split, flat, flat),
        check_vma=False,
    )
```

```python
import jax
import jax.numpy as jnp
from jax import lax
from jax.experimental import pallas as pl
from jax.experimental.pallas import tpu as pltpu
from jax.sharding import PartitionSpec as P

NEG_WEIGHT = 0.0625
LEARN_RATE = 0.1
F32, BF16, I32 = jnp.float32, jnp.bfloat16, jnp.int32
LANES = 128
ODD, EVEN = 1, 0
VMEM = pl.BlockSpec(memory_space=pltpu.VMEM)
SMEM = pl.BlockSpec(memory_space=pltpu.SMEM)
HBM = pl.BlockSpec(memory_space=pltpu.HBM)
NN, NT, TN = ((1,), (0,)), ((1,), (1,)), ((0,), (0,))


def role():
    return lax.rem(lax.axis_index("blk"), 2)


def dot(a, b, dims):
    return lax.dot_general(a, b, (dims, ((), ())), preferred_element_type=F32)


def hi_lo(x):
    hi = x.astype(BF16)
    return hi, (x - hi.astype(F32)).astype(BF16)


def cols(s):
    return pl.ds(s * LANES, LANES)


def one_hot(rows):
    which = lax.broadcasted_iota(I32, (LANES, LANES), 0)
    parts = [jnp.where(rows[r : r + 1, :] == which, 1.0, 0.0).astype(BF16) for r in range(rows.shape[0])]
    return jnp.concatenate(parts, axis=1)


def make_labels(labels_ref, he, te, tasks):
    for s in range(tasks):
        labels_ref[s] = dot(one_hot(te[s]), one_hot(he[s]), NT)


def rel_copies(rel_ids, rel_ref, rel_buf, sem, step, tasks):
    copies = []
    for s in range(tasks):
        start = pl.multiple_of((rel_ids[step, 0, s] // LANES) * LANES, LANES)
        copies.append(pltpu.make_async_copy(rel_ref.at[:, pl.ds(start, LANES)], rel_buf.at[s], sem.at[s]))
    return copies


def edge_copies(he_hbm, te_hbm, he, te, sem, step, tasks):
    rows = pl.ds(step * tasks, tasks)
    return [pltpu.make_async_copy(he_hbm.at[rows], he, sem.at[0]), pltpu.make_async_copy(te_hbm.at[rows], te, sem.at[1])]


def scale_heads(head, rel_ids, count, rel_buf, step, shi, slo, rel_out, live, tasks):
    for s in range(tasks):
        lane = lax.rem(rel_ids[step, 0, s], LANES)
        pick = (lax.broadcasted_iota(I32, (LANES, LANES), 0) == lane).astype(F32).astype(BF16)
        rel = dot(rel_buf[s], pick, NN)
        rel_out[:, cols(s)] = rel.astype(BF16)
        shi[:, cols(s)], slo[:, cols(s)] = hi_lo(head * rel)
        live[s] = jnp.full(live.shape[1:], jnp.where(s < count, 1.0, 0.0), F32)


def adagrad(block, state, grad):
    state = state + jnp.sum(grad * grad, axis=0, keepdims=True) * (1.0 / block.shape[0])
    return block - grad * (LEARN_RATE / jnp.sqrt(state)), state


def tail_step(tail, state, shi_ref, slo_ref, labels_ref, live_ref, kept, tail_out, tasks):
    thi_ref, tlo_ref, chi_ref, clo_ref = kept
    width = tail.shape[0]
    thi, tlo = hi_lo(tail)
    thi_ref[...], tlo_ref[...] = thi, tlo
    shi, slo = shi_ref[...], slo_ref[...]
    scores = dot(thi, shi, TN) + dot(tlo, shi, TN) + dot(thi, slo, TN)
    for s in range(tasks):
        score = scores[:, s * LANES : (s + 1) * LANES]
        coefficient = NEG_WEIGHT * (0.5 * jnp.tanh(0.5 * score) + 0.5) - labels_ref[s]
        chi_ref[:, cols(s)], clo_ref[:, cols(s)] = hi_lo(coefficient * live_ref[s, 0:1, :])
    chi, clo = chi_ref[...], clo_ref[...]
    grad = dot(shi, chi, NT) + dot(slo, chi, NT) + dot(shi, clo, NT)
    tail, state = adagrad(tail, state, grad)
    tail_out[pl.ds(0, width), :] = tail
    tail_out[pl.ds(width, 8), :] = jnp.broadcast_to(state, (8, LANES))


def head_step(head, state, kept, rel_ref, tasks):
    thi_ref, tlo_ref, chi_ref, clo_ref = kept
    thi, tlo = thi_ref[...], tlo_ref[...]
    grad = None
    for s in range(tasks):
        chi, clo = chi_ref[:, cols(s)], clo_ref[:, cols(s)]
        term = dot(thi, chi, NN) + dot(tlo, chi, NN) + dot(thi, clo, NN)
        term = term * rel_ref[:, cols(s)].astype(F32)
        grad = term if grad is None else grad + term
    return adagrad(head, state, grad)


def first_kernel(mine, tasks):
    n = 11

    def body(counts_hbm, ids_hbm, head_hbm, tail_hbm, hacc_hbm, tacc_hbm, rel_ref, he_hbm, te_hbm, *refs):
        outs, scratch = refs[-9 - n - 1 : -9], refs[-9:]
        tail_out, kept, (head, hacc, shi, slo, labels_ref, rel_out, live) = outs[0], outs[1:5], outs[5:]
        counts, rel_ids, tail, tacc, he, te, rel_buf, rel_sem, sem = scratch

        @pl.when(role() == mine)
        def _():
            small = [pltpu.make_async_copy(counts_hbm, counts, sem.at[2]), pltpu.make_async_copy(ids_hbm, rel_ids, sem.at[3])]
            edges = edge_copies(he_hbm, te_hbm, he, te, sem, 0, tasks)
            blocks = [pltpu.make_async_copy(src, dst, sem.at[4 + i]) for i, (src, dst) in enumerate(
                ((head_hbm, head), (tail_hbm, tail), (hacc_hbm, hacc), (tacc_hbm, tacc)))]
            for copy in small + edges + blocks:
                copy.start()
            for copy in small:
                copy.wait()
            rels = rel_copies(rel_ids, rel_ref, rel_buf, rel_sem, 0, tasks)
            for copy in rels:
                copy.start()
            for copy in edges:
                copy.wait()
            make_labels(labels_ref, he, te, tasks)
            for copy in rels + blocks:
                copy.wait()
            scale_heads(head[...], rel_ids, counts[0, 0], rel_buf, 0, shi, slo, rel_out, live, tasks)
            tail_step(tail[...], tacc[...], shi, slo, labels_ref, live, kept, tail_out, tasks)

    return body


def tail_kernel(mine, tasks, width):
    def body(tail_in, shi, slo, labels_ref, live, *refs):
        outs = refs[4:]

        @pl.when(role() == mine)
        def _():
            tail, state = tail_in[pl.ds(0, width), :], tail_in[pl.ds(width, 1), :]
            tail_step(tail, state, shi, slo, labels_ref, live, outs[1:5], outs[0], tasks)

    return body


def head_kernel(m, tasks, rounds):
    def body(counts, rel_ids, rel_ref, he_hbm, te_hbm, thi, tlo, chi, clo, *refs):
        ins, outs, (he, te, rel_buf, rel_sem, sem) = refs[:7], refs[7:14], refs[14:]
        head, hacc, rel_in = ins[0], ins[1], ins[5]
        head_out, hacc_out, shi, slo, labels_ref, rel_out, live = outs
        done = m - 1 + role()

        @pl.when((done >= 0) & (done < rounds - 1))
        def _():
            step = done + 1
            rels = rel_copies(rel_ids, rel_ref, rel_buf, rel_sem, step, tasks)
            edges = edge_copies(he_hbm, te_hbm, he, te, sem, step, tasks)
            for copy in edges + rels:
                copy.start()
            new, state = head_step(head[...], hacc[...], (thi, tlo, chi, clo), rel_in, tasks)
            head_out[...] = new
            hacc_out[...] = state
            for copy in edges:
                copy.wait()
            make_labels(labels_ref, he, te, tasks)
            for copy in rels:
                copy.wait()
            scale_heads(new, rel_ids, counts[0, step], rel_buf, step, shi, slo, rel_out, live, tasks)

    return body


def last_heads(tasks):
    def body(head, hacc, rel_in, thi, tlo, chi, clo, head_out, hacc_out):
        head_out[...], hacc_out[...] = head_step(head[...], hacc[...], (thi, tlo, chi, clo), rel_in, tasks)

    return body


def pick_tails(width):
    def body(from_odd, from_even, tail_out, tacc_out):
        for mine, ref in ((EVEN, from_odd), (ODD, from_even)):
            @pl.when(role() == mine)
            def _():
                tail_out[...] = ref[pl.ds(0, width), :]
                tacc_out[...] = ref[pl.ds(width, 1), :]

    return body


def call(body, ins, outs, scratch, args, name, alias=None):
    args = [pltpu.with_memory_space_constraint(a, pltpu.HBM) if spec is HBM else a for spec, a in zip(ins, args)]
    return pl.pallas_call(
        body,
        in_specs=ins,
        out_specs=[VMEM] * len(outs),
        out_shape=[jax.ShapeDtypeStruct(*o) for o in outs],
        scratch_shapes=scratch,
        input_output_aliases=alias or {},
        compiler_params=pltpu.CompilerParams(vmem_limit_bytes=16 << 20),
        cost_estimate=pl.CostEstimate(flops=10**9, bytes_accessed=1 << 20, transcendentals=0),
        name=name,
    )(*args)


def send(block, distance, mine):
    n = lax.axis_size("blk")
    return lax.ppermute(block, "blk", [(i, (i + distance) % n) for i in range(mine, n, 2)])


def swap(block):
    return lax.ppermute(block, "blk", [(i, i ^ 1) for i in range(lax.axis_size("blk"))])


def on_device(heads, tails, head_acc, tail_acc, relations, counts, rel_ids, head_edges, tail_edges):
    rounds, _, tasks, edges = head_edges.shape
    rows, width = heads.shape
    head, tail, rels = heads.T, tails.T, relations.T
    hacc, tacc, counts = head_acc.reshape(1, rows), tail_acc.reshape(1, rows), counts.T
    he = head_edges.reshape(rounds * tasks, edges // LANES, LANES)
    te = tail_edges.reshape(rounds * tasks, edges // LANES, LANES)
    wide = tasks * rows
    block, packed, row = ((width, rows), F32), ((width + 8, rows), F32), ((1, rows), F32)
    coeff, scaled, table = ((rows, wide), BF16), ((width, wide), BF16), ((tasks, rows, rows), F32)
    half, mask = ((width, rows), BF16), ((tasks, 8, rows), F32)
    kept_shapes = [half, half, coeff, coeff]
    state_shapes = [block, row, scaled, scaled, table, scaled, mask]
    edge_buf = pltpu.VMEM((tasks, edges // LANES, LANES), I32)
    rel_scratch = [pltpu.VMEM((tasks, width, LANES), BF16), pltpu.SemaphoreType.DMA((tasks,))]

    def first(mine, carried):
        return call(
            first_kernel(mine, tasks), [HBM] * 9 + [VMEM] * len(carried), [packed] + kept_shapes + state_shapes,
            [pltpu.SMEM(counts.shape, I32), pltpu.SMEM(rel_ids.shape, I32), pltpu.VMEM(*block), pltpu.VMEM(*row),
             edge_buf, edge_buf] + rel_scratch + [pltpu.SemaphoreType.DMA((8,))],
            [counts, rel_ids, head, tail, hacc, tacc, rels, he, te] + carried, f"first_{mine}",
            {9 + i: 1 + i for i in range(len(carried))})

    def tails_step(mine, k, tail_in, kept, state):
        out = call(
            tail_kernel(mine, tasks, width), [VMEM] * 9, [packed] + kept_shapes, [],
            [tail_in, state[2], state[3], state[4], state[6]] + kept, f"tails_{k}_{mine}",
            {5 + i: 1 + i for i in range(4)})
        return out[0], list(out[1:])

    def heads_step(m, kept, state):
        return list(call(
            head_kernel(m, tasks, rounds), [SMEM, SMEM, HBM, HBM, HBM] + [VMEM] * 11, state_shapes,
            [edge_buf, edge_buf] + rel_scratch + [pltpu.SemaphoreType.DMA((2,))],
            [counts, rel_ids, rels, he, te] + kept + state, f"heads_{m}", {9 + i: i for i in range(7)}))

    out = first(ODD, [])
    to_even = send(out[0], 1, ODD)
    out = first(EVEN, list(out[1:]))
    own, kept, state = out[0], list(out[1:5]), list(out[5:])
    state = heads_step(0, kept, state)
    for k in range(1, rounds):
        to_odd = swap(own)
        own, kept = tails_step(ODD, k, to_odd, kept, state)
        arrived = to_even
        to_even = send(own, 1 if k < rounds - 1 else 1 - rounds, ODD)
        state = heads_step(k, kept, state)
        own, kept = tails_step(EVEN, k, arrived, kept, state)
    to_odd = send(own, 1 - rounds, EVEN)
    head, hacc = call(last_heads(tasks), [VMEM] * 7, [block, row], [], [state[0], state[1], state[5]] + kept, "heads_last")
    tail, tacc = call(pick_tails(width), [VMEM] * 2, [block, row], [], [to_even, to_odd], "pick_tails")
    return head.T, tail.T, hacc.reshape(rows), tacc.reshape(rows)


def solution(mesh):
    split, edge = P(("blk", "help"), None), P(None, ("blk", "help"), None, None)
    flat = P(("blk", "help"))
    return jax.shard_map(
        on_device,
        mesh=mesh,
        in_specs=(split, split, flat, flat, P(), P(None, ("blk", "help")), P(None, ("blk", "help"), None), edge, edge),
        out_specs=(split, split, flat, flat),
        check_vma=False,
    )
```

```python
import jax
import jax.numpy as jnp
from jax import lax
from jax.experimental import pallas as pl
from jax.experimental.pallas import tpu as pltpu
from jax.sharding import PartitionSpec as P


NEG_WEIGHT = 0.0625
LEARN_RATE = 0.1
F32, BF16, I32 = jnp.float32, jnp.bfloat16, jnp.int32
LANES = 128
ODD, EVEN = 1, 0
VMEM = pl.BlockSpec(memory_space=pltpu.VMEM)
SMEM = pl.BlockSpec(memory_space=pltpu.SMEM)
HBM = pl.BlockSpec(memory_space=pltpu.HBM)
NN, NT, TN = ((1,), (0,)), ((1,), (1,)), ((0,), (0,))


def role():
    return lax.rem(lax.axis_index("blk"), 2)


def dot(a, b, dims):
    return lax.dot_general(a, b, (dims, ((), ())), preferred_element_type=F32)


def hi_lo(x):
    hi = x.astype(BF16)
    return hi, (x - hi.astype(F32)).astype(BF16)


def cols(s):
    return pl.ds(s * LANES, LANES)


def one_hot(rows):
    which = lax.broadcasted_iota(I32, (LANES, LANES), 0)
    parts = [jnp.where(rows[r : r + 1, :] == which, 1.0, 0.0).astype(BF16) for r in range(rows.shape[0])]
    return jnp.concatenate(parts, axis=1)


def make_labels(labels_ref, he, te, tasks):
    for s in range(tasks):
        labels_ref[s] = dot(one_hot(te[s]), one_hot(he[s]), NT)


def rel_copies(rel_ids, rel_ref, rel_buf, sem, step, tasks):
    copies = []
    for s in range(tasks):
        start = pl.multiple_of((rel_ids[step, 0, s] // LANES) * LANES, LANES)
        copies.append(pltpu.make_async_copy(rel_ref.at[:, pl.ds(start, LANES)], rel_buf.at[s], sem.at[s]))
    return copies


def edge_copies(he_hbm, te_hbm, he, te, sem, step, tasks):
    rows = pl.ds(step * tasks, tasks)
    return [pltpu.make_async_copy(he_hbm.at[rows], he, sem.at[0]), pltpu.make_async_copy(te_hbm.at[rows], te, sem.at[1])]


def scale_heads(head, rel_ids, count, rel_buf, step, shi, slo, rel_out, live, tasks):
    for s in range(tasks):
        lane = lax.rem(rel_ids[step, 0, s], LANES)
        pick = (lax.broadcasted_iota(I32, (LANES, LANES), 0) == lane).astype(F32).astype(BF16)
        rel = dot(rel_buf[s], pick, NN)
        rel_out[:, cols(s)] = rel.astype(BF16)
        shi[:, cols(s)], slo[:, cols(s)] = hi_lo(head * rel)
        live[s] = jnp.full(live.shape[1:], jnp.where(s < count, 1.0, 0.0), F32)


def adagrad(block, state, grad):
    state = state + jnp.sum(grad * grad, axis=0, keepdims=True) * (1.0 / block.shape[0])
    return block - grad * (LEARN_RATE / jnp.sqrt(state)), state


def tail_step(tail, state, shi_ref, slo_ref, labels_ref, live_ref, kept, tail_out, tasks):
    thi_ref, tlo_ref, chi_ref, clo_ref = kept
    width = tail.shape[0]
    thi, tlo = hi_lo(tail)
    thi_ref[...], tlo_ref[...] = thi, tlo
    shi, slo = shi_ref[...], slo_ref[...]
    scores = dot(thi, shi, TN) + dot(tlo, shi, TN) + dot(thi, slo, TN)
    for s in range(tasks):
        score = scores[:, s * LANES : (s + 1) * LANES]
        coefficient = NEG_WEIGHT * (0.5 * jnp.tanh(0.5 * score) + 0.5) - labels_ref[s]
        chi_ref[:, cols(s)], clo_ref[:, cols(s)] = hi_lo(coefficient * live_ref[s, 0:1, :])
    chi, clo = chi_ref[...], clo_ref[...]
    grad = dot(shi, chi, NT) + dot(slo, chi, NT) + dot(shi, clo, NT)
    tail, state = adagrad(tail, state, grad)
    tail_out[pl.ds(0, width), :] = tail
    tail_out[pl.ds(width, 8), :] = jnp.broadcast_to(state, (8, LANES))


def head_step(head, state, kept, rel_ref, tasks):
    thi_ref, tlo_ref, chi_ref, clo_ref = kept
    thi, tlo = thi_ref[...], tlo_ref[...]
    grad = None
    for s in range(tasks):
        chi, clo = chi_ref[:, cols(s)], clo_ref[:, cols(s)]
        term = dot(thi, chi, NN) + dot(tlo, chi, NN) + dot(thi, clo, NN)
        term = term * rel_ref[:, cols(s)].astype(F32)
        grad = term if grad is None else grad + term
    return adagrad(head, state, grad)


def first_kernel(mine, tasks):
    n = 11

    def body(counts_hbm, ids_hbm, head_hbm, tail_hbm, hacc_hbm, tacc_hbm, rel_ref, he_hbm, te_hbm, *refs):
        outs, scratch = refs[-9 - n - 1 : -9], refs[-9:]
        tail_out, kept, (head, hacc, shi, slo, labels_ref, rel_out, live) = outs[0], outs[1:5], outs[5:]
        counts, rel_ids, tail, tacc, he, te, rel_buf, rel_sem, sem = scratch

        @pl.when(role() == mine)
        def _():
            small = [pltpu.make_async_copy(counts_hbm, counts, sem.at[2]), pltpu.make_async_copy(ids_hbm, rel_ids, sem.at[3])]
            edges = edge_copies(he_hbm, te_hbm, he, te, sem, 0, tasks)
            blocks = [pltpu.make_async_copy(src, dst, sem.at[4 + i]) for i, (src, dst) in enumerate(
                ((head_hbm, head), (tail_hbm, tail), (hacc_hbm, hacc), (tacc_hbm, tacc)))]
            for copy in small + edges + blocks:
                copy.start()
            for copy in small:
                copy.wait()
            rels = rel_copies(rel_ids, rel_ref, rel_buf, rel_sem, 0, tasks)
            for copy in rels:
                copy.start()
            for copy in edges:
                copy.wait()
            make_labels(labels_ref, he, te, tasks)
            for copy in rels + blocks:
                copy.wait()
            scale_heads(head[...], rel_ids, counts[0, 0], rel_buf, 0, shi, slo, rel_out, live, tasks)
            tail_step(tail[...], tacc[...], shi, slo, labels_ref, live, kept, tail_out, tasks)

    return body


def tail_kernel(mine, tasks, width):
    def body(tail_in, shi, slo, labels_ref, live, *refs):
        outs = refs[4:]

        @pl.when(role() == mine)
        def _():
            tail, state = tail_in[pl.ds(0, width), :], tail_in[pl.ds(width, 1), :]
            tail_step(tail, state, shi, slo, labels_ref, live, outs[1:5], outs[0], tasks)

    return body


def head_kernel(m, tasks, rounds):
    def body(counts, rel_ids, rel_ref, he_hbm, te_hbm, thi, tlo, chi, clo, *refs):
        ins, outs, (he, te, rel_buf, rel_sem, sem) = refs[:7], refs[7:14], refs[14:]
        head, hacc, rel_in = ins[0], ins[1], ins[5]
        head_out, hacc_out, shi, slo, labels_ref, rel_out, live = outs
        done = m - 1 + role()

        @pl.when((done >= 0) & (done < rounds - 1))
        def _():
            step = done + 1
            rels = rel_copies(rel_ids, rel_ref, rel_buf, rel_sem, step, tasks)
            edges = edge_copies(he_hbm, te_hbm, he, te, sem, step, tasks)
            for copy in edges + rels:
                copy.start()
            new, state = head_step(head[...], hacc[...], (thi, tlo, chi, clo), rel_in, tasks)
            head_out[...] = new
            hacc_out[...] = state
            for copy in edges:
                copy.wait()
            make_labels(labels_ref, he, te, tasks)
            for copy in rels:
                copy.wait()
            scale_heads(new, rel_ids, counts[0, step], rel_buf, step, shi, slo, rel_out, live, tasks)

    return body


def last_heads(tasks):
    def body(head, hacc, rel_in, thi, tlo, chi, clo, head_out, hacc_out):
        head_out[...], hacc_out[...] = head_step(head[...], hacc[...], (thi, tlo, chi, clo), rel_in, tasks)

    return body


def pick_tails(width):
    def body(from_odd, from_even, tail_out, tacc_out):
        for mine, ref in ((EVEN, from_odd), (ODD, from_even)):
            @pl.when(role() == mine)
            def _():
                tail_out[...] = ref[pl.ds(0, width), :]
                tacc_out[...] = ref[pl.ds(width, 1), :]

    return body


def call(body, ins, outs, scratch, args, alias=None):
    args = [pltpu.with_memory_space_constraint(a, pltpu.HBM) if spec is HBM else a for spec, a in zip(ins, args)]
    return pl.pallas_call(
        body,
        in_specs=ins,
        out_specs=[VMEM] * len(outs),
        out_shape=[jax.ShapeDtypeStruct(*o) for o in outs],
        scratch_shapes=scratch,
        input_output_aliases=alias or {},
        compiler_params=pltpu.CompilerParams(vmem_limit_bytes=16 << 20),
        cost_estimate=pl.CostEstimate(flops=10**9, bytes_accessed=1 << 20, transcendentals=0),
    )(*args)


def send(block, distance, mine):
    n = lax.axis_size("blk")
    return lax.ppermute(block, "blk", [(i, (i + distance) % n) for i in range(mine, n, 2)])


def swap(block):
    return lax.ppermute(block, "blk", [(i, i ^ 1) for i in range(lax.axis_size("blk"))])


def on_device(heads, tails, head_acc, tail_acc, relations, counts, rel_ids, head_edges, tail_edges):
    rounds, _, tasks, edges = head_edges.shape
    rows, width = heads.shape
    head, tail, rels = heads.T, tails.T, relations.T
    hacc, tacc, counts = head_acc.reshape(1, rows), tail_acc.reshape(1, rows), counts.T
    he = head_edges.reshape(rounds * tasks, edges // LANES, LANES)
    te = tail_edges.reshape(rounds * tasks, edges // LANES, LANES)
    wide = tasks * rows
    block, packed, row = ((width, rows), F32), ((width + 8, rows), F32), ((1, rows), F32)
    coeff, scaled, table = ((rows, wide), BF16), ((width, wide), BF16), ((tasks, rows, rows), F32)
    half, mask = ((width, rows), BF16), ((tasks, 8, rows), F32)
    kept_shapes = [half, half, coeff, coeff]
    state_shapes = [block, row, scaled, scaled, table, scaled, mask]
    edge_buf = pltpu.VMEM((tasks, edges // LANES, LANES), I32)
    rel_scratch = [pltpu.VMEM((tasks, width, LANES), BF16), pltpu.SemaphoreType.DMA((tasks,))]

    def first(mine, carried):
        return call(
            first_kernel(mine, tasks), [HBM] * 9 + [VMEM] * len(carried), [packed] + kept_shapes + state_shapes,
            [pltpu.SMEM(counts.shape, I32), pltpu.SMEM(rel_ids.shape, I32), pltpu.VMEM(*block), pltpu.VMEM(*row),
             edge_buf, edge_buf] + rel_scratch + [pltpu.SemaphoreType.DMA((8,))],
            [counts, rel_ids, head, tail, hacc, tacc, rels, he, te] + carried,
            {9 + i: 1 + i for i in range(len(carried))})

    def tails_step(mine, tail_in, kept, state):
        out = call(
            tail_kernel(mine, tasks, width), [VMEM] * 9, [packed] + kept_shapes, [],
            [tail_in, state[2], state[3], state[4], state[6]] + kept,
            {5 + i: 1 + i for i in range(4)})
        return out[0], list(out[1:])

    def heads_step(m, kept, state):
        return list(call(
            head_kernel(m, tasks, rounds), [SMEM, SMEM, HBM, HBM, HBM] + [VMEM] * 11, state_shapes,
            [edge_buf, edge_buf] + rel_scratch + [pltpu.SemaphoreType.DMA((2,))],
            [counts, rel_ids, rels, he, te] + kept + state, {9 + i: i for i in range(7)}))

    out = first(ODD, [])
    to_even = send(out[0], 1, ODD)
    out = first(EVEN, list(out[1:]))
    own, kept, state = out[0], list(out[1:5]), list(out[5:])
    to_odd = swap(own)
    state = heads_step(0, kept, state)
    for k in range(1, rounds):
        last = k == rounds - 1
        own, kept = tails_step(ODD, to_odd, kept, state)
        arrived = to_even
        to_even = send(own, 1 - rounds if last else 1, ODD)
        state = heads_step(k, kept, state)
        own, kept = tails_step(EVEN, arrived, kept, state)
        to_odd = send(own, 1 - rounds, EVEN) if last else swap(own)
    head, hacc = call(last_heads(tasks), [VMEM] * 7, [block, row], [], [state[0], state[1], state[5]] + kept)
    tail, tacc = call(pick_tails(width), [VMEM] * 2, [block, row], [], [to_even, to_odd])
    return head.T, tail.T, hacc.reshape(rows), tacc.reshape(rows)


def solution(mesh):
    split, edge = P(("blk", "help"), None), P(None, ("blk", "help"), None, None)
    flat = P(("blk", "help"))

    return jax.shard_map(
        on_device,
        mesh=mesh,
        in_specs=(split, split, flat, flat, P(), P(None, ("blk", "help")), P(None, ("blk", "help"), None), edge, edge),
        out_specs=(split, split, flat, flat),
        check_vma=False,
    )
```

```python
import jax
import jax.numpy as jnp
from jax import lax
from jax.experimental import pallas as pl
from jax.experimental.pallas import tpu as pltpu
from jax.sharding import PartitionSpec as P


NEG_WEIGHT = 0.0625
LEARN_RATE = 0.1
F32, BF16, I32 = jnp.float32, jnp.bfloat16, jnp.int32
LANES = 128
ODD, EVEN = 1, 0
VMEM = pl.BlockSpec(memory_space=pltpu.VMEM)
SMEM = pl.BlockSpec(memory_space=pltpu.SMEM)
HBM = pl.BlockSpec(memory_space=pltpu.HBM)
NN, NT, TN = ((1,), (0,)), ((1,), (1,)), ((0,), (0,))


def role():
    return lax.rem(lax.axis_index("blk"), 2)


def dot(a, b, dims):
    return lax.dot_general(a, b, (dims, ((), ())), preferred_element_type=F32)


def hi_lo(x):
    hi = x.astype(BF16)
    return hi, (x - hi.astype(F32)).astype(BF16)


def cols(s):
    return pl.ds(s * LANES, LANES)


def one_hot(rows):
    which = lax.broadcasted_iota(I32, (LANES, LANES), 0)
    parts = [jnp.where(rows[r : r + 1, :] == which, 1.0, 0.0).astype(BF16) for r in range(rows.shape[0])]
    return jnp.concatenate(parts, axis=1)


def make_labels(labels_ref, he, te, source, target, tasks):
    for s in range(tasks):
        labels_ref[target + s] = dot(one_hot(te[source + s]), one_hot(he[source + s]), NT)


def rel_copies(rel_ids, rel_ref, rel_buf, sem, k, tasks):
    copies = []
    for s in range(tasks):
        start = pl.multiple_of((rel_ids[k, 0, s] // LANES) * LANES, LANES)
        copies.append(pltpu.make_async_copy(rel_ref.at[:, pl.ds(start, LANES)], rel_buf.at[k * tasks + s], sem.at[k * tasks + s]))
    return copies


def scale_heads(head, lanes, rel_buf, k, shi, slo, rel_out, tasks):
    for s in range(tasks):
        pick = (lax.broadcasted_iota(I32, (LANES, LANES), 0) == lanes[k * tasks + s, 0:1, :]).astype(F32).astype(BF16)
        rel = dot(rel_buf[k * tasks + s], pick, NN)
        rel_out[:, cols(s)] = rel.astype(BF16)
        shi[:, cols(s)], slo[:, cols(s)] = hi_lo(head * rel)


def adagrad(block, state, grad):
    state = state + jnp.sum(grad * grad, axis=0, keepdims=True) * (1.0 / block.shape[0])
    return block - grad * (LEARN_RATE / jnp.sqrt(state)), state


def tail_step(tail, state, shi_ref, slo_ref, labels_ref, label_row, live_ref, live_row, kept, tail_out, tasks):
    thi_ref, tlo_ref, chi_ref, clo_ref = kept
    width = tail.shape[0]
    thi, tlo = hi_lo(tail)
    thi_ref[...], tlo_ref[...] = thi, tlo
    shi, slo = shi_ref[...], slo_ref[...]
    scores = dot(thi, shi, TN) + dot(tlo, shi, TN) + dot(thi, slo, TN)
    for s in range(tasks):
        score = scores[:, s * LANES : (s + 1) * LANES]
        coefficient = NEG_WEIGHT * (0.5 * jnp.tanh(0.5 * score) + 0.5) - labels_ref[label_row + s]
        chi_ref[:, cols(s)], clo_ref[:, cols(s)] = hi_lo(coefficient * live_ref[live_row + s, 0:1, :])
    chi, clo = chi_ref[...], clo_ref[...]
    grad = dot(shi, chi, NT) + dot(slo, chi, NT) + dot(shi, clo, NT)
    tail, state = adagrad(tail, state, grad)
    tail_out[pl.ds(0, width), :] = tail
    tail_out[pl.ds(width, 8), :] = jnp.broadcast_to(state, (8, LANES))


def head_step(head, state, kept, rel_ref, tasks):
    thi_ref, tlo_ref, chi_ref, clo_ref = kept
    thi, tlo = thi_ref[...], tlo_ref[...]
    grad = None
    for s in range(tasks):
        chi, clo = chi_ref[:, cols(s)], clo_ref[:, cols(s)]
        term = dot(thi, chi, NN) + dot(tlo, chi, NN) + dot(thi, clo, NN)
        term = term * rel_ref[:, cols(s)].astype(F32)
        grad = term if grad is None else grad + term
    return adagrad(head, state, grad)


def first_kernel(mine, tasks, rounds):
    n_out = 15

    def body(counts_hbm, ids_hbm, head_hbm, tail_hbm, hacc_hbm, tacc_hbm, rel_ref, he_hbm, te_hbm, *refs):
        outs, scratch = refs[-7 - n_out : -7], refs[-7:]
        tail_out, kept, (head, hacc, shi, slo, rel_out), (he, te, rel_buf, lanes, live) = outs[0], outs[1:5], outs[5:10], outs[10:]
        counts, rel_ids, tail, tacc, labels_ref, rel_sem, sem = scratch

        @pl.when(role() == mine)
        def _():
            pairs = ((ids_hbm, rel_ids), (counts_hbm, counts), (he_hbm, he), (te_hbm, te), (head_hbm, head), (tail_hbm, tail),
                     (hacc_hbm, hacc), (tacc_hbm, tacc))
            copies = [pltpu.make_async_copy(src, dst, sem.at[i]) for i, (src, dst) in enumerate(pairs)]
            for copy in copies:
                copy.start()
            copies[0].wait()
            rels = [rel_copies(rel_ids, rel_ref, rel_buf, rel_sem, k, tasks) for k in range(rounds)]
            for group in rels:
                for copy in group:
                    copy.start()
            for copy in copies[1:4]:
                copy.wait()
            make_labels(labels_ref, he, te, 0, 0, tasks)
            for k in range(rounds):
                for s in range(tasks):
                    lanes[k * tasks + s] = jnp.full(lanes.shape[1:], lax.rem(rel_ids[k, 0, s], LANES), I32)
                    live[k * tasks + s] = jnp.full(live.shape[1:], jnp.where(s < counts[0, k], 1.0, 0.0), F32)
            for copy in rels[0] + copies[4:]:
                copy.wait()
            scale_heads(head[...], lanes, rel_buf, 0, shi, slo, rel_out, tasks)
            tail_step(tail[...], tacc[...], shi, slo, labels_ref, 0, live, 0, kept, tail_out, tasks)
            for group in rels[1:]:
                for copy in group:
                    copy.wait()

    return body


def tail_kernel(mine, k, tasks, width):
    def body(tail_in, shi, slo, labels_ref, live, *refs):
        outs = refs[4:]

        @pl.when(role() == mine)
        def _():
            tail, state = tail_in[pl.ds(0, width), :], tail_in[pl.ds(width, 1), :]
            tail_step(tail, state, shi, slo, labels_ref, (k - 1) * tasks, live, k * tasks, outs[1:5], outs[0], tasks)

    return body


LABEL_ROUNDS = {(0, ODD): (1,), (1, ODD): (2, 3), (1, EVEN): (1, 2), (3, EVEN): (3,)}


def head_kernel(m, tasks, rounds):
    def body(he, te, rel_buf, lanes, thi, tlo, chi, clo, *refs):
        ins, (head_out, hacc_out, shi, slo, rel_out, labels_ref) = refs[:5], refs[-6:]
        head, hacc, rel_in = ins[0], ins[1], ins[4]
        for mine, done in ((ODD, m), (EVEN, m - 1)):
            if not 0 <= done < rounds - 1:
                continue

            @pl.when(role() == mine)
            def _():
                new, state = head_step(head[...], hacc[...], (thi, tlo, chi, clo), rel_in, tasks)
                head_out[...] = new
                hacc_out[...] = state
                scale_heads(new, lanes, rel_buf, done + 1, shi, slo, rel_out, tasks)
                for k in LABEL_ROUNDS.get((m, mine), ()):
                    make_labels(labels_ref, he, te, k * tasks, (k - 1) * tasks, tasks)

    return body


def last_heads(tasks):
    def body(head, hacc, rel_in, thi, tlo, chi, clo, head_out, hacc_out):
        head_out[...], hacc_out[...] = head_step(head[...], hacc[...], (thi, tlo, chi, clo), rel_in, tasks)

    return body


def pick_tails(width):
    def body(from_odd, from_even, tail_out, tacc_out):
        for mine, ref in ((EVEN, from_odd), (ODD, from_even)):
            @pl.when(role() == mine)
            def _():
                tail_out[...] = ref[pl.ds(0, width), :]
                tacc_out[...] = ref[pl.ds(width, 1), :]

    return body


def call(body, ins, outs, scratch, args, alias=None):
    args = [pltpu.with_memory_space_constraint(a, pltpu.HBM) if spec is HBM else a for spec, a in zip(ins, args)]
    return pl.pallas_call(
        body,
        in_specs=ins,
        out_specs=[VMEM] * len(outs),
        out_shape=[jax.ShapeDtypeStruct(*o) for o in outs],
        scratch_shapes=scratch,
        input_output_aliases=alias or {},
        compiler_params=pltpu.CompilerParams(vmem_limit_bytes=16 << 20),
        cost_estimate=pl.CostEstimate(flops=10**9, bytes_accessed=1 << 20, transcendentals=0),
    )(*args)


def send(block, distance, mine):
    n = lax.axis_size("blk")
    return lax.ppermute(block, "blk", [(i, (i + distance) % n) for i in range(mine, n, 2)])


def send_or_swap(block, distance, mine):
    n = lax.axis_size("blk")
    return lax.ppermute(block, "blk", [(i, (i + distance) % n if i % 2 == mine else i ^ 1) for i in range(n)])


def on_device(heads, tails, head_acc, tail_acc, relations, counts, rel_ids, head_edges, tail_edges):
    rounds, _, tasks, edges = head_edges.shape
    rows, width = heads.shape
    head, tail, rels = heads.T, tails.T, relations.T
    hacc, tacc, counts = head_acc.reshape(1, rows), tail_acc.reshape(1, rows), counts.T
    slots, groups, wide = rounds * tasks, edges // LANES, tasks * rows
    he, te = head_edges.reshape(slots, groups, LANES), tail_edges.reshape(slots, groups, LANES)
    block, packed, row = ((width, rows), F32), ((width + 8, rows), F32), ((1, rows), F32)
    coeff, scaled, half = ((rows, wide), BF16), ((width, wide), BF16), ((width, rows), BF16)
    table = ((slots - tasks, rows, rows), F32)
    kept_shapes = [half, half, coeff, coeff]
    state_shapes = [block, row, scaled, scaled, scaled]
    edge = ((slots, groups, LANES), I32)
    fixed_shapes = [edge, edge, ((slots, width, LANES), BF16), ((slots, 8, rows), I32), ((slots, 8, rows), F32)]

    def first(mine, carried):
        return call(
            first_kernel(mine, tasks, rounds), [HBM] * 9 + [VMEM] * len(carried),
            [packed] + kept_shapes + state_shapes + fixed_shapes,
            [pltpu.SMEM(counts.shape, I32), pltpu.SMEM(rel_ids.shape, I32), pltpu.VMEM(*block), pltpu.VMEM(*row),
             pltpu.VMEM((tasks, rows, rows), F32), pltpu.SemaphoreType.DMA((slots,)), pltpu.SemaphoreType.DMA((8,))],
            [counts, rel_ids, head, tail, hacc, tacc, rels, he, te] + carried,
            {9 + i: 1 + i for i in range(len(carried))})

    def tails_step(mine, k, tail_in, kept, state):
        out = call(
            tail_kernel(mine, k, tasks, width), [VMEM] * 9, [packed] + kept_shapes, [],
            [tail_in, state[2], state[3], state[5], fixed[4]] + kept, {5 + i: 1 + i for i in range(4)})
        return out[0], list(out[1:])

    def heads_step(m, kept, state):
        return list(call(
            head_kernel(m, tasks, rounds), [VMEM] * (8 + len(state)), state_shapes + [table], [],
            list(fixed[:4]) + kept + state, {8 + i: i for i in range(len(state))}))

    out = first(ODD, [])
    to_even = send(out[0], 1, ODD)
    out = first(EVEN, list(out[1:]))
    own, kept, state, fixed = out[0], list(out[1:5]), list(out[5:10]), list(out[10:])
    to_odd = send_or_swap(own, 1, EVEN)
    state = heads_step(0, kept, state)
    for k in range(1, rounds):
        distance = 1 if k < rounds - 1 else 1 - rounds
        own, kept = tails_step(ODD, k, to_odd, kept, state)
        arrived = to_even
        to_even = send_or_swap(own, distance, ODD)
        state = heads_step(k, kept, state)
        own, kept = tails_step(EVEN, k, arrived, kept, state)
        to_odd = send_or_swap(own, distance, EVEN)
    head, hacc = call(last_heads(tasks), [VMEM] * 7, [block, row], [], [state[0], state[1], state[4]] + kept)
    tail, tacc = call(pick_tails(width), [VMEM] * 2, [block, row], [], [to_even, to_odd])
    return head.T, tail.T, hacc.reshape(rows), tacc.reshape(rows)


def solution(mesh):
    split, edge = P(("blk", "help"), None), P(None, ("blk", "help"), None, None)
    flat = P(("blk", "help"))

    return jax.shard_map(
        on_device,
        mesh=mesh,
        in_specs=(split, split, flat, flat, P(), P(None, ("blk", "help")), P(None, ("blk", "help"), None), edge, edge),
        out_specs=(split, split, flat, flat),
        check_vma=False,
    )
```

```python
import jax
import jax.numpy as jnp
from jax import lax
from jax.experimental import pallas as pl
from jax.experimental.pallas import tpu as pltpu
from jax.sharding import PartitionSpec as P


HALF_NEG = 0.0625 / 2
LEARN_RATE = 0.1
F32, BF16, I32 = jnp.float32, jnp.bfloat16, jnp.int32
LANES = 128
ODD, EVEN = 1, 0
VMEM = pl.BlockSpec(memory_space=pltpu.VMEM)
SMEM = pl.BlockSpec(memory_space=pltpu.SMEM)
HBM = pl.BlockSpec(memory_space=pltpu.HBM)
NN, NT, TN = ((1,), (0,)), ((1,), (1,)), ((0,), (0,))


def role():
    return lax.rem(lax.axis_index("blk"), 2)


def dot(a, b, dims):
    return lax.dot_general(a, b, (dims, ((), ())), preferred_element_type=F32)


def hi_lo(x):
    hi = x.astype(BF16)
    return hi, (x - hi.astype(F32)).astype(BF16)


def cols(s):
    return pl.ds(s * LANES, LANES)


def one_hot(rows):
    which = lax.broadcasted_iota(I32, (LANES, LANES), 0)
    parts = [jnp.where(rows[r : r + 1, :] == which, 1.0, 0.0).astype(BF16) for r in range(rows.shape[0])]
    return jnp.concatenate(parts, axis=1)


def make_labels(labels_ref, he, te, gain, source, target, tasks):
    for s in range(tasks):
        count = dot(one_hot(te[source + s]), one_hot(he[source + s]), NT)
        labels_ref[target + s] = gain[source + s, 0:1, :] * (1.0 - count * (1.0 / HALF_NEG))


def rel_copies(rel_ids, rel_ref, rel_buf, sem, k, tasks):
    copies = []
    for s in range(tasks):
        start = pl.multiple_of((rel_ids[k, 0, s] // LANES) * LANES, LANES)
        copies.append(pltpu.make_async_copy(rel_ref.at[:, pl.ds(start, LANES)], rel_buf.at[k * tasks + s], sem.at[k * tasks + s]))
    return copies


def scale_heads(head, lanes, rel_buf, k, shi, slo, rel_out, tasks):
    for s in range(tasks):
        pick = (lax.broadcasted_iota(I32, (LANES, LANES), 0) == lanes[k * tasks + s, 0:1, :]).astype(F32).astype(BF16)
        rel = dot(rel_buf[k * tasks + s], pick, NN)
        rel_out[:, cols(s)] = rel.astype(BF16)
        shi[:, cols(s)], slo[:, cols(s)] = hi_lo(head * rel)


def adagrad(block, state, grad):
    width = block.shape[0]
    square, part = grad * grad, width // 5
    square = (square[:part] + square[part : 2 * part]) + (square[2 * part : 3 * part] + square[3 * part : 4 * part]) + square[4 * part :]
    state = state + jnp.sum(square, axis=0, keepdims=True) * (1.0 / width)
    return block - grad * (LEARN_RATE / jnp.sqrt(state)), state


def tail_step(tail, state, shi_ref, slo_ref, labels_ref, label_row, gain_ref, gain_row, kept, tail_outs, tasks):
    thi_ref, tlo_ref, chi_ref, clo_ref = kept
    width = tail.shape[0]
    thi, tlo = hi_lo(tail)
    thi_ref[...], tlo_ref[...] = thi, tlo
    shi, slo = shi_ref[...], slo_ref[...]
    both = dot(jnp.concatenate([thi, tlo], axis=1), shi, TN)
    scores = both[:LANES] + both[LANES:] + dot(thi, slo, TN)
    for s in range(tasks):
        score = scores[:, s * LANES : (s + 1) * LANES]
        coefficient = gain_ref[gain_row + s, 0:1, :] * jnp.tanh(0.5 * score) + labels_ref[label_row + s]
        chi_ref[:, cols(s)], clo_ref[:, cols(s)] = hi_lo(coefficient)
    chi, clo = chi_ref[...], clo_ref[...]
    both = dot(shi, jnp.concatenate([chi, clo], axis=0), NT)
    grad = both[:, :LANES] + both[:, LANES:] + dot(slo, chi, NT)
    tail, state = adagrad(tail, state, grad)
    whole = ((0, width, tail), (width, 8, jnp.broadcast_to(state, (8, LANES))))
    start = 0
    for ref in tail_outs:
        stop = start + ref.shape[0]
        for first, size, value in whole:
            lo, hi = max(start, first), min(stop, first + size)
            if lo < hi:
                ref[pl.ds(lo - start, hi - lo), :] = value[lo - first : hi - first]
        start = stop


def head_step(head, state, kept, rel_ref, tasks):
    thi_ref, tlo_ref, chi_ref, clo_ref = kept
    thi, tlo, chi = thi_ref[...], tlo_ref[...], chi_ref[...]
    wide = dot(jnp.concatenate([thi, tlo], axis=1), jnp.concatenate([chi, chi], axis=0), NN) + dot(thi, clo_ref[...], NN)
    grad = None
    for s in range(tasks):
        term = wide[:, s * LANES : (s + 1) * LANES] * rel_ref[:, cols(s)].astype(F32)
        grad = term if grad is None else grad + term
    return adagrad(head, state, grad)


def first_kernel(mine, tasks, rounds):
    n_sent = 2 if mine == ODD else 1
    n_out = 14 + n_sent

    def body(counts_hbm, ids_hbm, head_hbm, tail_hbm, hacc_hbm, tacc_hbm, rel_ref, he_hbm, te_hbm, *refs):
        outs, scratch = refs[-7 - n_out : -7], refs[-7:]
        sent, outs = outs[:n_sent], outs[n_sent:]
        kept, (head, hacc, shi, slo, rel_out), (he, te, rel_buf, lanes, gain) = outs[:4], outs[4:9], outs[9:]
        counts, rel_ids, tail, tacc, labels_ref, rel_sem, sem = scratch

        @pl.when(role() == mine)
        def _():
            pairs = ((ids_hbm, rel_ids), (counts_hbm, counts), (he_hbm, he), (te_hbm, te), (head_hbm, head), (tail_hbm, tail),
                     (hacc_hbm, hacc), (tacc_hbm, tacc))
            copies = [pltpu.make_async_copy(src, dst, sem.at[i]) for i, (src, dst) in enumerate(pairs)]
            for copy in copies:
                copy.start()
            copies[0].wait()
            rels = [rel_copies(rel_ids, rel_ref, rel_buf, rel_sem, k, tasks) for k in range(rounds)]
            for copy in rels[0]:
                copy.start()
            for copy in copies[1:4]:
                copy.wait()
            for k in range(rounds):
                for s in range(tasks):
                    lanes[k * tasks + s] = jnp.full(lanes.shape[1:], lax.rem(rel_ids[k, 0, s], LANES), I32)
                    gain[k * tasks + s] = jnp.full(gain.shape[1:], jnp.where(s < counts[0, k], HALF_NEG, 0.0), F32)
            make_labels(labels_ref, he, te, gain, 0, 0, tasks)
            for group in rels[1:]:
                for copy in group:
                    copy.start()
            for copy in rels[0] + copies[4:]:
                copy.wait()
            scale_heads(head[...], lanes, rel_buf, 0, shi, slo, rel_out, tasks)
            tail_step(tail[...], tacc[...], shi, slo, labels_ref, 0, gain, 0, kept, sent, tasks)
            for group in rels[1:]:
                for copy in group:
                    copy.wait()

    return body


def tail_kernel(mine, k, tasks, width, n_in):
    def body(*refs):
        tail_in, (shi, slo, labels_ref, gain), outs = refs[:n_in], refs[n_in : n_in + 4], refs[n_in + 8 :]

        @pl.when(role() == mine)
        def _():
            tail = jnp.concatenate([ref[...] for ref in tail_in], axis=0) if n_in > 1 else tail_in[0][...]
            tail_step(tail[:width], tail[width : width + 1], shi, slo, labels_ref, (k - 1) * tasks, gain, k * tasks, outs[1:5], outs[:1], tasks)

    return body


LABEL_ROUNDS = {(0, ODD): (1,), (1, ODD): (2, 3), (1, EVEN): (1, 2), (3, EVEN): (3,)}


def head_kernel(mine, m, tasks):
    done = m if mine == ODD else m - 1

    def body(he, te, rel_buf, lanes, gain, thi, tlo, chi, clo, *refs):
        ins, (head_out, hacc_out, shi, slo, rel_out, labels_ref) = refs[:5], refs[-6:]
        head, hacc, rel_in = ins[0], ins[1], ins[4]

        @pl.when(role() == mine)
        def _():
            new, state = head_step(head[...], hacc[...], (thi, tlo, chi, clo), rel_in, tasks)
            head_out[...] = new
            hacc_out[...] = state
            scale_heads(new, lanes, rel_buf, done + 1, shi, slo, rel_out, tasks)
            for k in LABEL_ROUNDS.get((m, mine), ()):
                make_labels(labels_ref, he, te, gain, k * tasks, (k - 1) * tasks, tasks)

    return body


def last_heads(tasks):
    def body(head, hacc, rel_in, thi, tlo, chi, clo, head_out, hacc_out):
        head_out[...], hacc_out[...] = head_step(head[...], hacc[...], (thi, tlo, chi, clo), rel_in, tasks)

    return body


def pick_tails(width):
    def body(from_odd, from_even, tail_out, tacc_out):
        for mine, ref in ((EVEN, from_odd), (ODD, from_even)):
            @pl.when(role() == mine)
            def _():
                tail_out[...] = ref[pl.ds(0, width), :]
                tacc_out[...] = ref[pl.ds(width, 1), :]

    return body


def call(body, ins, outs, scratch, args, alias=None):
    args = [pltpu.with_memory_space_constraint(a, pltpu.HBM) if spec is HBM else a for spec, a in zip(ins, args)]
    return pl.pallas_call(
        body,
        in_specs=ins,
        out_specs=[VMEM] * len(outs),
        out_shape=[jax.ShapeDtypeStruct(*o) for o in outs],
        scratch_shapes=scratch,
        input_output_aliases=alias or {},
        compiler_params=pltpu.CompilerParams(vmem_limit_bytes=16 << 20),
        cost_estimate=pl.CostEstimate(flops=10**9, bytes_accessed=1 << 20, transcendentals=0),
    )(*args)


def send(block, distance, mine):
    n = lax.axis_size("blk")
    return lax.ppermute(block, "blk", [(i, (i + distance) % n) for i in range(mine, n, 2)])


def send_or_swap(block, distance, mine):
    n = lax.axis_size("blk")
    return lax.ppermute(block, "blk", [(i, (i + distance) % n if i % 2 == mine else i ^ 1) for i in range(n)])


def on_device(heads, tails, head_acc, tail_acc, relations, counts, rel_ids, head_edges, tail_edges):
    rounds, _, tasks, edges = head_edges.shape
    rows, width = heads.shape
    head, tail, rels = heads.T, tails.T, relations.T
    hacc, tacc, counts = head_acc.reshape(1, rows), tail_acc.reshape(1, rows), counts.T
    slots, groups, wide = rounds * tasks, edges // LANES, tasks * rows
    he, te = head_edges.reshape(slots, groups, LANES), tail_edges.reshape(slots, groups, LANES)
    block, packed, row = ((width, rows), F32), ((width + 8, rows), F32), ((1, rows), F32)
    coeff, scaled, half = ((rows, wide), BF16), ((width, wide), BF16), ((width, rows), BF16)
    table = ((slots - tasks, rows, rows), F32)
    kept_shapes = [half, half, coeff, coeff]
    state_shapes = [block, row, scaled, scaled, scaled]
    edge = ((slots, groups, LANES), I32)
    fixed_shapes = [edge, edge, ((slots, width, LANES), BF16), ((slots, 8, rows), I32), ((slots, 8, rows), F32)]

    halves = [((width // 2, rows), F32), ((width - width // 2 + 8, rows), F32)]

    def first(mine, carried):
        sent = halves if mine == ODD else [packed]
        return call(
            first_kernel(mine, tasks, rounds), [HBM] * 9 + [VMEM] * len(carried),
            sent + kept_shapes + state_shapes + fixed_shapes,
            [pltpu.SMEM(counts.shape, I32), pltpu.SMEM(rel_ids.shape, I32), pltpu.VMEM(*block), pltpu.VMEM(*row),
             pltpu.VMEM((tasks, rows, rows), F32), pltpu.SemaphoreType.DMA((slots,)), pltpu.SemaphoreType.DMA((8,))],
            [counts, rel_ids, head, tail, hacc, tacc, rels, he, te] + carried,
            {9 + i: len(sent) + i for i in range(len(carried))})

    def tails_step(mine, k, tail_in, kept, state):
        n = len(tail_in)
        out = call(
            tail_kernel(mine, k, tasks, width, n), [VMEM] * (n + 8), [packed] + kept_shapes, [],
            tail_in + [state[2], state[3], state[5], fixed[4]] + kept, {n + 4 + i: 1 + i for i in range(4)})
        return out[0], list(out[1:])

    def heads_step(mine, m, kept, state):
        return list(call(
            head_kernel(mine, m, tasks), [VMEM] * (9 + len(state)), state_shapes + [table], [],
            list(fixed) + kept + state, {9 + i: i for i in range(len(state))}))

    out = list(first(ODD, []))
    to_even = []
    for i in range(2):
        to_even.append(send(out[i], 1, ODD))
    out = first(EVEN, out[2:])
    own, kept, state, fixed = out[0], list(out[1:5]), list(out[5:10]), list(out[10:])
    to_odd = send_or_swap(own, 1, EVEN)
    state = heads_step(ODD, 0, kept, state)
    for k in range(1, rounds):
        distance = 1 if k < rounds - 1 else 1 - rounds
        own, kept = tails_step(ODD, k, [to_odd], kept, state)
        arrived = to_even
        to_even = [send_or_swap(own, distance, ODD)]
        if k < rounds - 1:
            state = heads_step(ODD, k, kept, state)
        state = heads_step(EVEN, k, kept, state)
        own, kept = tails_step(EVEN, k, arrived, kept, state)
        to_odd = send_or_swap(own, distance, EVEN)
    head, hacc = call(last_heads(tasks), [VMEM] * 7, [block, row], [], [state[0], state[1], state[4]] + kept)
    tail, tacc = call(pick_tails(width), [VMEM] * 2, [block, row], [], [to_even[0], to_odd])
    return head.T, tail.T, hacc.reshape(rows), tacc.reshape(rows)


def solution(mesh):
    split, edge = P(("blk", "help"), None), P(None, ("blk", "help"), None, None)
    flat = P(("blk", "help"))

    return jax.shard_map(
        on_device,
        mesh=mesh,
        in_specs=(split, split, flat, flat, P(), P(None, ("blk", "help")), P(None, ("blk", "help"), None), edge, edge),
        out_specs=(split, split, flat, flat),
        check_vma=False,
    )
```

```python
import jax
import jax.numpy as jnp
from jax import lax
from jax.experimental import pallas as pl
from jax.experimental.pallas import tpu as pltpu
from jax.sharding import PartitionSpec as P


HALF_NEG = 0.0625 / 2
LEARN_RATE = 0.1
F32, BF16, I32 = jnp.float32, jnp.bfloat16, jnp.int32
LANES = 128
ODD, EVEN = 1, 0
VMEM = pl.BlockSpec(memory_space=pltpu.VMEM)
SMEM = pl.BlockSpec(memory_space=pltpu.SMEM)
HBM = pl.BlockSpec(memory_space=pltpu.HBM)
NN, NT, TN = ((1,), (0,)), ((1,), (1,)), ((0,), (0,))


def role():
    return lax.rem(lax.axis_index("blk"), 2)


def dot(a, b, dims):
    return lax.dot_general(a, b, (dims, ((), ())), preferred_element_type=F32)


def hi_lo(x):
    hi = x.astype(BF16)
    return hi, (x - hi.astype(F32)).astype(BF16)


def cols(s):
    return pl.ds(s * LANES, LANES)


def one_hot(rows):
    which = lax.broadcasted_iota(I32, (LANES, LANES), 0).astype(F32).astype(BF16)
    one, zero = jnp.ones((), BF16), jnp.zeros((), BF16)
    parts = []
    for r in range(rows.shape[0]):
        row = jnp.broadcast_to(rows[r : r + 1, :].astype(F32), (16, LANES)).astype(BF16)
        parts.append(jnp.where(which == jnp.concatenate([row] * (LANES // 16), axis=0), one, zero))
    return jnp.concatenate(parts, axis=1)


def make_labels(labels_ref, he, te, gain, source, target, tasks):
    for s in range(tasks):
        count = dot(one_hot(te[source + s]), one_hot(he[source + s]), NT)
        labels_ref[target + s] = gain[source + s, 0:1, :] * (1.0 - count * (1.0 / HALF_NEG))


def rel_copies(rel_ids, rel_ref, rel_buf, sem, k, tasks):
    copies = []
    for s in range(tasks):
        start = pl.multiple_of((rel_ids[k, 0, s] // LANES) * LANES, LANES)
        copies.append(pltpu.make_async_copy(rel_ref.at[:, pl.ds(start, LANES)], rel_buf.at[k * tasks + s], sem.at[k * tasks + s]))
    return copies


def scale_heads(head, lanes, rel_buf, k, shi, slo, rel_out, tasks):
    for s in range(tasks):
        pick = (lax.broadcasted_iota(I32, (LANES, LANES), 0) == lanes[k * tasks + s, 0:1, :]).astype(F32).astype(BF16)
        rel = dot(rel_buf[k * tasks + s], pick, NN)
        rel_out[:, cols(s)] = rel.astype(BF16)
        shi[:, cols(s)], slo[:, cols(s)] = hi_lo(head * rel)


def adagrad(block, state, grad):
    width = block.shape[0]
    square, part = grad * grad, width // 5
    square = (square[:part] + square[part : 2 * part]) + (square[2 * part : 3 * part] + square[3 * part : 4 * part]) + square[4 * part :]
    state = state + jnp.sum(square, axis=0, keepdims=True) * (1.0 / width)
    return block - grad * (LEARN_RATE / jnp.sqrt(state)), state


def tail_step(tail, state, shi_ref, slo_ref, labels_ref, label_row, gain_ref, gain_row, kept, tail_out, tasks):
    thi_ref, tlo_ref, chi_ref, clo_ref = kept
    width = tail.shape[0]
    thi, tlo = hi_lo(tail)
    thi_ref[...], tlo_ref[...] = thi, tlo
    shi, slo = shi_ref[...], slo_ref[...]
    both = dot(jnp.concatenate([thi, tlo], axis=1), shi, TN)
    scores = both[:LANES] + both[LANES:] + dot(thi, slo, TN)
    for s in range(tasks):
        score = scores[:, s * LANES : (s + 1) * LANES]
        coefficient = gain_ref[gain_row + s, 0:1, :] * jnp.tanh(0.5 * score) + labels_ref[label_row + s]
        chi_ref[:, cols(s)], clo_ref[:, cols(s)] = hi_lo(coefficient)
    chi, clo = chi_ref[...], clo_ref[...]
    both = dot(shi, jnp.concatenate([chi, clo], axis=0), NT)
    grad = both[:, :LANES] + both[:, LANES:] + dot(slo, chi, NT)
    tail, state = adagrad(tail, state, grad)
    tail_out[pl.ds(0, width), :] = tail
    tail_out[pl.ds(width, 8), :] = jnp.broadcast_to(state, (8, LANES))


def head_step(head, state, kept, rel_ref, tasks):
    thi_ref, tlo_ref, chi_ref, clo_ref = kept
    thi, tlo, chi = thi_ref[...], tlo_ref[...], chi_ref[...]
    wide = dot(jnp.concatenate([thi, tlo], axis=1), jnp.concatenate([chi, chi], axis=0), NN) + dot(thi, clo_ref[...], NN)
    grad = None
    for s in range(tasks):
        term = wide[:, s * LANES : (s + 1) * LANES] * rel_ref[:, cols(s)].astype(F32)
        grad = term if grad is None else grad + term
    return adagrad(head, state, grad)


def first_kernel(tasks, rounds, width):
    def body(counts_hbm, ids_hbm, head_hbm, tail_hbm, hacc_hbm, tacc_hbm, rel_ref, he_hbm, te_hbm, *refs):
        outs, (counts, rel_ids, tacc, rel_sem, sem) = refs[:16], refs[16:]
        tail_out, (head, hacc, shi, slo, rel_out, labels_ref), (he, te, rel_buf, lanes, gain) = outs[0], outs[5:11], outs[11:]
        pairs = ((ids_hbm, rel_ids), (counts_hbm, counts), (he_hbm, he), (te_hbm, te), (head_hbm, head),
                 (tail_hbm, tail_out.at[pl.ds(0, width)]), (hacc_hbm, hacc), (tacc_hbm, tacc))
        copies = [pltpu.make_async_copy(src, dst, sem.at[i]) for i, (src, dst) in enumerate(pairs)]
        for copy in copies:
            copy.start()
        copies[0].wait()
        rels = [rel_copies(rel_ids, rel_ref, rel_buf, rel_sem, k, tasks) for k in range(rounds)]
        for copy in rels[0]:
            copy.start()
        for copy in copies[1:4]:
            copy.wait()
        for k in range(rounds):
            for s in range(tasks):
                lanes[k * tasks + s] = jnp.full(lanes.shape[1:], lax.rem(rel_ids[k, 0, s], LANES), I32)
                gain[k * tasks + s] = jnp.full(gain.shape[1:], jnp.where(s < counts[0, k], HALF_NEG, 0.0), F32)
        make_labels(labels_ref, he, te, gain, 0, 0, tasks)
        for group in rels[1:]:
            for copy in group:
                copy.start()
        for copy in rels[0] + copies[4:]:
            copy.wait()
        tail_out[pl.ds(width, 8), :] = jnp.broadcast_to(tacc[...], (8, LANES))
        scale_heads(head[...], lanes, rel_buf, 0, shi, slo, rel_out, tasks)
        for group in rels[1:]:
            for copy in group:
                copy.wait()

    return body


def tail_kernel(mine, k, tasks, width):
    def body(tail_in, shi, slo, labels_ref, gain, *refs):
        outs = refs[4:]

        @pl.when(role() == mine)
        def _():
            tail, state = tail_in[pl.ds(0, width), :], tail_in[pl.ds(width, 1), :]
            tail_step(tail, state, shi, slo, labels_ref, k * tasks, gain, k * tasks, outs[1:5], outs[0], tasks)

    return body


LABEL_ROUNDS = {(0, ODD): (1,), (1, ODD): (2, 3), (1, EVEN): (1, 2), (3, EVEN): (3,)}


def head_kernel(mine, m, tasks):
    done = m if mine == ODD else m - 1

    def body(he, te, rel_buf, lanes, gain, thi, tlo, chi, clo, *refs):
        ins, (head_out, hacc_out, shi, slo, rel_out, labels_ref) = refs[:5], refs[-6:]
        head, hacc, rel_in = ins[0], ins[1], ins[4]

        @pl.when(role() == mine)
        def _():
            new, state = head_step(head[...], hacc[...], (thi, tlo, chi, clo), rel_in, tasks)
            head_out[...] = new
            hacc_out[...] = state
            scale_heads(new, lanes, rel_buf, done + 1, shi, slo, rel_out, tasks)
            for k in LABEL_ROUNDS.get((m, mine), ()):
                make_labels(labels_ref, he, te, gain, k * tasks, k * tasks, tasks)

    return body


def last_heads(tasks):
    def body(head, hacc, rel_in, thi, tlo, chi, clo, head_out, hacc_out):
        head_out[...], hacc_out[...] = head_step(head[...], hacc[...], (thi, tlo, chi, clo), rel_in, tasks)

    return body


def pick_tails(width):
    def body(from_odd, from_even, tail_out, tacc_out):
        for mine, ref in ((EVEN, from_odd), (ODD, from_even)):
            @pl.when(role() == mine)
            def _():
                tail_out[...] = ref[pl.ds(0, width), :]
                tacc_out[...] = ref[pl.ds(width, 1), :]

    return body


def call(body, ins, outs, scratch, args, alias=None):
    args = [pltpu.with_memory_space_constraint(a, pltpu.HBM) if spec is HBM else a for spec, a in zip(ins, args)]
    return pl.pallas_call(
        body,
        in_specs=ins,
        out_specs=[VMEM] * len(outs),
        out_shape=[jax.ShapeDtypeStruct(*o) for o in outs],
        scratch_shapes=scratch,
        input_output_aliases=alias or {},
        compiler_params=pltpu.CompilerParams(vmem_limit_bytes=16 << 20),
        cost_estimate=pl.CostEstimate(flops=10**9, bytes_accessed=1 << 20, transcendentals=0),
    )(*args)


def send_or_swap(block, distance, mine):
    n = lax.axis_size("blk")
    return lax.ppermute(block, "blk", [(i, (i + distance) % n if i % 2 == mine else i ^ 1) for i in range(n)])


def on_device(heads, tails, head_acc, tail_acc, relations, counts, rel_ids, head_edges, tail_edges):
    rounds, _, tasks, edges = head_edges.shape
    rows, width = heads.shape
    head, tail, rels = heads.T, tails.T, relations.T
    hacc, tacc, counts = head_acc.reshape(1, rows), tail_acc.reshape(1, rows), counts.T
    slots, groups, wide = rounds * tasks, edges // LANES, tasks * rows
    he, te = head_edges.reshape(slots, groups, LANES), tail_edges.reshape(slots, groups, LANES)
    block, packed, row = ((width, rows), F32), ((width + 8, rows), F32), ((1, rows), F32)
    coeff, scaled, half = ((rows, wide), BF16), ((width, wide), BF16), ((width, rows), BF16)
    table = ((slots, rows, rows), F32)
    kept_shapes = [half, half, coeff, coeff]
    state_shapes = [block, row, scaled, scaled, scaled, table]
    edge = ((slots, groups, LANES), I32)
    fixed_shapes = [edge, edge, ((slots, width, LANES), BF16), ((slots, 8, rows), I32), ((slots, 8, rows), F32)]

    def tails_step(mine, k, tail_in, kept, state):
        out = call(
            tail_kernel(mine, k, tasks, width), [VMEM] * 9, [packed] + kept_shapes, [],
            [tail_in, state[2], state[3], state[5], fixed[4]] + kept, {5 + i: 1 + i for i in range(4)})
        return out[0], list(out[1:])

    def heads_step(mine, m, kept, state):
        return list(call(
            head_kernel(mine, m, tasks), [VMEM] * 15, state_shapes, [],
            list(fixed) + kept + state, {9 + i: i for i in range(6)}))

    out = call(
        first_kernel(tasks, rounds, width), [HBM] * 9, [packed] + kept_shapes + state_shapes + fixed_shapes,
        [pltpu.SMEM(counts.shape, I32), pltpu.SMEM(rel_ids.shape, I32), pltpu.VMEM(*row),
         pltpu.SemaphoreType.DMA((slots,)), pltpu.SemaphoreType.DMA((8,))],
        [counts, rel_ids, head, tail, hacc, tacc, rels, he, te])
    start, kept, state, fixed = out[0], list(out[1:5]), list(out[5:11]), list(out[11:])
    own, kept = tails_step(ODD, 0, start, kept, state)
    to_even = send_or_swap(own, 1, ODD)
    own, kept = tails_step(EVEN, 0, start, kept, state)
    to_odd = send_or_swap(own, 1, EVEN)
    state = heads_step(ODD, 0, kept, state)
    for k in range(1, rounds):
        distance = 1 if k < rounds - 1 else 1 - rounds
        own, kept = tails_step(ODD, k, to_odd, kept, state)
        arrived = to_even
        to_even = send_or_swap(own, distance, ODD)
        if k < rounds - 1:
            state = heads_step(ODD, k, kept, state)
        state = heads_step(EVEN, k, kept, state)
        own, kept = tails_step(EVEN, k, arrived, kept, state)
        to_odd = send_or_swap(own, distance, EVEN)
    head, hacc = call(last_heads(tasks), [VMEM] * 7, [block, row], [], [state[0], state[1], state[4]] + kept)
    tail, tacc = call(pick_tails(width), [VMEM] * 2, [block, row], [], [to_even, to_odd])
    return head.T, tail.T, hacc.reshape(rows), tacc.reshape(rows)


def solution(mesh):
    split, edge = P(("blk", "help"), None), P(None, ("blk", "help"), None, None)
    flat = P(("blk", "help"))

    return jax.shard_map(
        on_device,
        mesh=mesh,
        in_specs=(split, split, flat, flat, P(), P(None, ("blk", "help")), P(None, ("blk", "help"), None), edge, edge),
        out_specs=(split, split, flat, flat),
        check_vma=False,
    )
```

```python
import jax
import jax.numpy as jnp
from jax import lax
from jax.experimental import pallas as pl
from jax.experimental.pallas import tpu as pltpu
from jax.sharding import PartitionSpec as P


HALF_NEG = 0.0625 / 2
LEARN_RATE = 0.1
F32, BF16, I32 = jnp.float32, jnp.bfloat16, jnp.int32
LANES = 128
ODD, EVEN = 1, 0
VMEM = pl.BlockSpec(memory_space=pltpu.VMEM)
SMEM = pl.BlockSpec(memory_space=pltpu.SMEM)
HBM = pl.BlockSpec(memory_space=pltpu.HBM)
NN, NT, TN = ((1,), (0,)), ((1,), (1,)), ((0,), (0,))


def role():
    return lax.rem(lax.axis_index("blk"), 2)


def dot(a, b, dims):
    return lax.dot_general(a, b, (dims, ((), ())), preferred_element_type=F32)


def hi_lo(x):
    hi = x.astype(BF16)
    return hi, (x - hi.astype(F32)).astype(BF16)


def cols(s):
    return pl.ds(s * LANES, LANES)


def one_hot(rows):
    which = lax.broadcasted_iota(I32, (LANES, LANES), 0).astype(F32).astype(BF16)
    one, zero = jnp.ones((), BF16), jnp.zeros((), BF16)
    parts = []
    for r in range(rows.shape[0]):
        row = jnp.broadcast_to(rows[r : r + 1, :].astype(F32), (16, LANES)).astype(BF16)
        parts.append(jnp.where(which == jnp.concatenate([row] * (LANES // 16), axis=0), one, zero))
    return jnp.concatenate(parts, axis=1)


def make_labels(labels_ref, he, te, gain, source, target, tasks):
    for s in range(tasks):
        count = dot(one_hot(te[source + s]), one_hot(he[source + s]), NT)
        labels_ref[target + s] = gain[source + s, 0:1, :] * (1.0 - count * (1.0 / HALF_NEG))


def rel_copies(rel_ids, rel_ref, rel_buf, sem, k, tasks):
    copies = []
    for s in range(tasks):
        start = pl.multiple_of((rel_ids[k, 0, s] // LANES) * LANES, LANES)
        copies.append(pltpu.make_async_copy(rel_ref.at[:, pl.ds(start, LANES)], rel_buf.at[k * tasks + s], sem.at[k * tasks + s]))
    return copies


def scale_heads(head, lanes, rel_buf, k, shi, slo, rel_out, tasks):
    for s in range(tasks):
        pick = (lax.broadcasted_iota(I32, (LANES, LANES), 0) == lanes[k * tasks + s, 0:1, :]).astype(F32).astype(BF16)
        rel = dot(rel_buf[k * tasks + s], pick, NN)
        rel_out[:, cols(s)] = rel.astype(BF16)
        shi[:, cols(s)], slo[:, cols(s)] = hi_lo(head * rel)


def adagrad(block, state, grad):
    width = block.shape[0]
    square, part = grad * grad, width // 5
    square = (square[:part] + square[part : 2 * part]) + (square[2 * part : 3 * part] + square[3 * part : 4 * part]) + square[4 * part :]
    state = state + jnp.sum(square, axis=0, keepdims=True) * (1.0 / width)
    return block - grad * (LEARN_RATE / jnp.sqrt(state)), state


def tail_step(tail, state, shi_ref, slo_ref, labels_ref, label_row, gain_ref, gain_row, kept, tail_out, tasks):
    thi_ref, tlo_ref, chi_ref, clo_ref = kept
    width = tail.shape[0]
    thi, tlo = hi_lo(tail)
    thi_ref[...], tlo_ref[...] = thi, tlo
    shi, slo = shi_ref[...], slo_ref[...]
    both = dot(jnp.concatenate([thi, tlo], axis=1), shi, TN)
    scores = both[:LANES] + both[LANES:] + dot(thi, slo, TN)
    for s in range(tasks):
        score = scores[:, s * LANES : (s + 1) * LANES]
        coefficient = gain_ref[gain_row + s, 0:1, :] * jnp.tanh(0.5 * score) + labels_ref[label_row + s]
        chi_ref[:, cols(s)], clo_ref[:, cols(s)] = hi_lo(coefficient)
    chi, clo = chi_ref[...], clo_ref[...]
    both = dot(shi, jnp.concatenate([chi, clo], axis=0), NT)
    grad = both[:, :LANES] + both[:, LANES:] + dot(slo, chi, NT)
    tail, state = adagrad(tail, state, grad)
    tail_out[pl.ds(0, width), :] = tail
    tail_out[pl.ds(width, 8), :] = jnp.broadcast_to(state, (8, LANES))


def head_step(head, state, kept, rel_ref, tasks):
    thi_ref, tlo_ref, chi_ref, clo_ref = kept
    thi, tlo, chi = thi_ref[...], tlo_ref[...], chi_ref[...]
    wide = dot(jnp.concatenate([thi, tlo], axis=1), jnp.concatenate([chi, chi], axis=0), NN) + dot(thi, clo_ref[...], NN)
    grad = None
    for s in range(tasks):
        term = wide[:, s * LANES : (s + 1) * LANES] * rel_ref[:, cols(s)].astype(F32)
        grad = term if grad is None else grad + term
    return adagrad(head, state, grad)


def first_kernel(tasks, rounds, width):
    def body(counts_hbm, ids_hbm, head_hbm, tail_hbm, hacc_hbm, tacc_hbm, rel_ref, he_hbm, te_hbm, *refs):
        outs, (counts, rel_ids, tacc, rel_sem, sem) = refs[:16], refs[16:]
        tail_out, (head, hacc, shi, slo, rel_out, labels_ref), (he, te, rel_buf, lanes, gain) = outs[0], outs[5:11], outs[11:]
        pairs = ((ids_hbm, rel_ids), (counts_hbm, counts), (he_hbm, he), (te_hbm, te), (head_hbm, head),
                 (tail_hbm, tail_out.at[pl.ds(0, width)]), (hacc_hbm, hacc), (tacc_hbm, tacc))
        copies = [pltpu.make_async_copy(src, dst, sem.at[i]) for i, (src, dst) in enumerate(pairs)]
        for copy in copies:
            copy.start()
        copies[0].wait()
        rels = [rel_copies(rel_ids, rel_ref, rel_buf, rel_sem, k, tasks) for k in range(rounds)]
        for group in rels:
            for copy in group:
                copy.start()
        for copy in copies[1:4]:
            copy.wait()
        for k in range(rounds):
            for s in range(tasks):
                lanes[k * tasks + s] = jnp.full(lanes.shape[1:], lax.rem(rel_ids[k, 0, s], LANES), I32)
                gain[k * tasks + s] = jnp.full(gain.shape[1:], jnp.where(s < counts[0, k], HALF_NEG, 0.0), F32)
        make_labels(labels_ref, he, te, gain, 0, 0, tasks)
        for copy in rels[0] + copies[4:]:
            copy.wait()
        tail_out[pl.ds(width, 8), :] = jnp.broadcast_to(tacc[...], (8, LANES))
        scale_heads(head[...], lanes, rel_buf, 0, shi, slo, rel_out, tasks)
        for group in rels[1:]:
            for copy in group:
                copy.wait()

    return body


def tail_kernel(mine, k, tasks, width):
    def body(tail_in, shi, slo, labels_ref, gain, *refs):
        outs = refs[4:]

        @pl.when(role() == mine)
        def _():
            tail, state = tail_in[pl.ds(0, width), :], tail_in[pl.ds(width, 1), :]
            tail_step(tail, state, shi, slo, labels_ref, k * tasks, gain, k * tasks, outs[1:5], outs[0], tasks)

    return body


LABEL_ROUNDS = {(0, ODD): (1,), (1, ODD): (2, 3), (1, EVEN): (1, 2), (3, EVEN): (3,)}


def head_kernel(mine, m, tasks):
    done = m if mine == ODD else m - 1

    def body(he, te, rel_buf, lanes, gain, thi, tlo, chi, clo, *refs):
        ins, (head_out, hacc_out, shi, slo, rel_out, labels_ref) = refs[:5], refs[-6:]
        head, hacc, rel_in = ins[0], ins[1], ins[4]

        @pl.when(role() == mine)
        def _():
            new, state = head_step(head[...], hacc[...], (thi, tlo, chi, clo), rel_in, tasks)
            head_out[...] = new
            hacc_out[...] = state
            scale_heads(new, lanes, rel_buf, done + 1, shi, slo, rel_out, tasks)
            for k in LABEL_ROUNDS.get((m, mine), ()):
                make_labels(labels_ref, he, te, gain, k * tasks, k * tasks, tasks)

    return body


def last_heads(tasks):
    def body(head, hacc, rel_in, thi, tlo, chi, clo, head_out, hacc_out):
        head_out[...], hacc_out[...] = head_step(head[...], hacc[...], (thi, tlo, chi, clo), rel_in, tasks)

    return body


def pick_tails(mine, width):
    def body(packed, *refs):
        tail_out, tacc_out, row, sem = refs[-4:]

        @pl.when(role() == mine)
        def _():
            row[...] = packed[pl.ds(width, 1), :]
            copies = [pltpu.make_async_copy(packed.at[pl.ds(0, width)], tail_out, sem.at[0]), pltpu.make_async_copy(row, tacc_out, sem.at[1])]
            for copy in copies:
                copy.start()
            for copy in copies:
                copy.wait()

    return body


def call(body, ins, outs, scratch, args, alias=None):
    args = [pltpu.with_memory_space_constraint(a, pltpu.HBM) if spec is HBM else a for spec, a in zip(ins, args)]
    return pl.pallas_call(
        body,
        in_specs=ins,
        out_specs=[VMEM] * len(outs),
        out_shape=[jax.ShapeDtypeStruct(*o) for o in outs],
        scratch_shapes=scratch,
        input_output_aliases=alias or {},
        compiler_params=pltpu.CompilerParams(vmem_limit_bytes=16 << 20),
        cost_estimate=pl.CostEstimate(flops=10**9, bytes_accessed=1 << 20, transcendentals=0),
    )(*args)


def send_or_swap(block, distance, mine):
    n = lax.axis_size("blk")
    return lax.ppermute(block, "blk", [(i, (i + distance) % n if i % 2 == mine else i ^ 1) for i in range(n)])


def on_device(heads, tails, head_acc, tail_acc, relations, counts, rel_ids, head_edges, tail_edges):
    rounds, _, tasks, edges = head_edges.shape
    rows, width = heads.shape
    head, tail, rels = heads.T, tails.T, relations.T
    hacc, tacc, counts = head_acc.reshape(1, rows), tail_acc.reshape(1, rows), counts.T
    slots, groups, wide = rounds * tasks, edges // LANES, tasks * rows
    he, te = head_edges.reshape(slots, groups, LANES), tail_edges.reshape(slots, groups, LANES)
    block, packed, row = ((width, rows), F32), ((width + 8, rows), F32), ((1, rows), F32)
    coeff, scaled, half = ((rows, wide), BF16), ((width, wide), BF16), ((width, rows), BF16)
    table = ((slots, rows, rows), F32)
    kept_shapes = [half, half, coeff, coeff]
    state_shapes = [block, row, scaled, scaled, scaled, table]
    edge = ((slots, groups, LANES), I32)
    fixed_shapes = [edge, edge, ((slots, width, LANES), BF16), ((slots, 8, rows), I32), ((slots, 8, rows), F32)]

    def tails_step(mine, k, tail_in, kept, state):
        out = call(
            tail_kernel(mine, k, tasks, width), [VMEM] * 9, [packed] + kept_shapes, [],
            [tail_in, state[2], state[3], state[5], fixed[4]] + kept, {5 + i: 1 + i for i in range(4)})
        return out[0], list(out[1:])

    def heads_step(mine, m, kept, state):
        return list(call(
            head_kernel(mine, m, tasks), [VMEM] * 15, state_shapes, [],
            list(fixed) + kept + state, {9 + i: i for i in range(6)}))

    out = call(
        first_kernel(tasks, rounds, width), [HBM] * 9, [packed] + kept_shapes + state_shapes + fixed_shapes,
        [pltpu.SMEM(counts.shape, I32), pltpu.SMEM(rel_ids.shape, I32), pltpu.VMEM(*row),
         pltpu.SemaphoreType.DMA((slots,)), pltpu.SemaphoreType.DMA((8,))],
        [counts, rel_ids, head, tail, hacc, tacc, rels, he, te])
    start, kept, state, fixed = out[0], list(out[1:5]), list(out[5:11]), list(out[11:])
    own, kept = tails_step(ODD, 0, start, kept, state)
    to_even = send_or_swap(own, 1, ODD)
    own, kept = tails_step(EVEN, 0, start, kept, state)
    to_odd = send_or_swap(own, 1, EVEN)
    state = heads_step(ODD, 0, kept, state)
    for k in range(1, rounds):
        distance = 1 if k < rounds - 1 else 1 - rounds
        own, kept = tails_step(ODD, k, to_odd, kept, state)
        arrived = to_even
        to_even = send_or_swap(own, distance, ODD)
        if k < rounds - 1:
            state = heads_step(ODD, k, kept, state)
        state = heads_step(EVEN, k, kept, state)
        own, kept = tails_step(EVEN, k, arrived, kept, state)
        to_odd = send_or_swap(own, distance, EVEN)
    head, hacc = call(last_heads(tasks), [VMEM] * 7, [block, row], [], [state[0], state[1], state[4]] + kept)
    results = []
    for mine, packed_in in ((EVEN, to_even), (ODD, to_odd)):
        results = pl.pallas_call(
            pick_tails(mine, width),
            in_specs=[VMEM] + [HBM] * len(results),
            out_specs=[HBM] * 2,
            out_shape=[pltpu.HBM(*block), pltpu.HBM(*row)],
            scratch_shapes=[pltpu.VMEM(*row), pltpu.SemaphoreType.DMA((2,))],
            input_output_aliases={1 + i: i for i in range(len(results))},
            compiler_params=pltpu.CompilerParams(vmem_limit_bytes=16 << 20),
        )(packed_in, *results)
    tail, tacc = results
    return head.T, tail.T, hacc.reshape(rows), tacc.reshape(rows)


def solution(mesh):
    split, edge = P(("blk", "help"), None), P(None, ("blk", "help"), None, None)
    flat = P(("blk", "help"))

    return jax.shard_map(
        on_device,
        mesh=mesh,
        in_specs=(split, split, flat, flat, P(), P(None, ("blk", "help")), P(None, ("blk", "help"), None), edge, edge),
        out_specs=(split, split, flat, flat),
        check_vma=False,
    )
```

```python
import jax
import jax.numpy as jnp
from jax import lax
from jax.experimental import pallas as pl
from jax.experimental.pallas import tpu as pltpu
from jax.sharding import PartitionSpec as P


HALF_NEG = 0.0625 / 2
LEARN_RATE = 0.1
F32, BF16, I32 = jnp.float32, jnp.bfloat16, jnp.int32
LANES = 128
ODD, EVEN = 1, 0
VMEM = pl.BlockSpec(memory_space=pltpu.VMEM)
SMEM = pl.BlockSpec(memory_space=pltpu.SMEM)
HBM = pl.BlockSpec(memory_space=pltpu.HBM)
NN, NT, TN = ((1,), (0,)), ((1,), (1,)), ((0,), (0,))


def role():
    return lax.rem(lax.axis_index("blk"), 2)


def dot(a, b, dims):
    return lax.dot_general(a, b, (dims, ((), ())), preferred_element_type=F32)


def hi_lo(x):
    hi = x.astype(BF16)
    return hi, (x - hi.astype(F32)).astype(BF16)


def cols(s):
    return pl.ds(s * LANES, LANES)


def one_hot(rows):
    which = lax.broadcasted_iota(I32, (LANES, LANES), 0).astype(F32).astype(BF16)
    one, zero = jnp.ones((), BF16), jnp.zeros((), BF16)
    parts = []
    for r in range(rows.shape[0]):
        row = jnp.broadcast_to(rows[r : r + 1, :].astype(F32), (16, LANES)).astype(BF16)
        parts.append(jnp.where(which == jnp.concatenate([row] * (LANES // 16), axis=0), one, zero))
    return jnp.concatenate(parts, axis=1)


def make_labels(labels_ref, he, te, gain, source, target, tasks):
    for s in range(tasks):
        count = dot(one_hot(te[source + s]), one_hot(he[source + s]), NT)
        labels_ref[target + s] = gain[source + s, 0:1, :] * (1.0 - count * (1.0 / HALF_NEG))


def rel_copies(rel_ids, rel_ref, rel_buf, sem, k, tasks):
    copies = []
    for s in range(tasks):
        start = pl.multiple_of((rel_ids[k, 0, s] // LANES) * LANES, LANES)
        copies.append(pltpu.make_async_copy(rel_ref.at[:, pl.ds(start, LANES)], rel_buf.at[k * tasks + s], sem.at[k * tasks + s]))
    return copies


def scale_heads(head, lanes, rel_buf, k, shi, slo, rel_out, tasks):
    which = lax.broadcasted_iota(I32, (LANES, LANES), 0)
    for first in range(0, tasks, 2):
        group = range(first, min(first + 2, tasks))
        picks = [(which == lanes[k * tasks + s, 0:1, :]).astype(F32).astype(BF16) for s in group]
        if len(group) == 2:
            none = jnp.zeros_like(picks[0])
            pick = jnp.concatenate([jnp.concatenate([picks[0], none], axis=1), jnp.concatenate([none, picks[1]], axis=1)], axis=0)
        else:
            pick = picks[0]
        rel = dot(jnp.concatenate([rel_buf[k * tasks + s] for s in group], axis=1), pick, NN)
        for i, s in enumerate(group):
            part = rel[:, i * LANES : (i + 1) * LANES]
            rel_out[:, cols(s)] = part.astype(BF16)
            shi[:, cols(s)], slo[:, cols(s)] = hi_lo(head * part)


def adagrad(block, state, grad):
    width = block.shape[0]
    square, part = grad * grad, width // 5
    square = (square[:part] + square[part : 2 * part]) + (square[2 * part : 3 * part] + square[3 * part : 4 * part]) + square[4 * part :]
    state = state + jnp.sum(square, axis=0, keepdims=True) * (1.0 / width)
    return block - grad * (LEARN_RATE * lax.rsqrt(state)), state


def tail_step(tail, state, shi_ref, slo_ref, labels_ref, label_row, gain_ref, gain_row, kept, tail_out, tasks):
    thi_ref, tlo_ref, chi_ref, clo_ref = kept
    width = tail.shape[0]
    thi, tlo = hi_lo(tail)
    thi_ref[...], tlo_ref[...] = thi, tlo
    shi, slo = shi_ref[...], slo_ref[...]
    both = dot(jnp.concatenate([thi, tlo], axis=1), shi, TN)
    scores = both[:LANES] + both[LANES:] + dot(thi, slo, TN)
    for s in range(tasks):
        score = scores[:, s * LANES : (s + 1) * LANES]
        coefficient = gain_ref[gain_row + s, 0:1, :] * jnp.tanh(0.5 * score) + labels_ref[label_row + s]
        chi_ref[:, cols(s)], clo_ref[:, cols(s)] = hi_lo(coefficient)
    chi, clo = chi_ref[...], clo_ref[...]
    both = dot(shi, jnp.concatenate([chi, clo], axis=0), NT)
    grad = both[:, :LANES] + both[:, LANES:] + dot(slo, chi, NT)
    tail, state = adagrad(tail, state, grad)
    tail_out[pl.ds(0, width), :] = tail
    tail_out[pl.ds(width, 8), :] = jnp.broadcast_to(state, (8, LANES))


def head_step(head, state, kept, rel_ref, tasks):
    thi_ref, tlo_ref, chi_ref, clo_ref = kept
    thi, tlo, chi = thi_ref[...], tlo_ref[...], chi_ref[...]
    wide = dot(jnp.concatenate([thi, tlo], axis=1), jnp.concatenate([chi, chi], axis=0), NN) + dot(thi, clo_ref[...], NN)
    grad = None
    for s in range(tasks):
        term = wide[:, s * LANES : (s + 1) * LANES] * rel_ref[:, cols(s)].astype(F32)
        grad = term if grad is None else grad + term
    return adagrad(head, state, grad)


def first_kernel(tasks, rounds, width):
    def body(counts_hbm, ids_hbm, head_hbm, tail_hbm, hacc_hbm, tacc_hbm, rel_ref, he_hbm, te_hbm, *refs):
        outs, (counts, rel_ids, tacc, rel_sem, sem) = refs[:16], refs[16:]
        tail_out, (head, hacc, shi, slo, rel_out, labels_ref), (he, te, rel_buf, lanes, gain) = outs[0], outs[5:11], outs[11:]
        pairs = ((ids_hbm, rel_ids), (counts_hbm, counts), (he_hbm, he), (te_hbm, te), (head_hbm, head),
                 (tail_hbm, tail_out.at[pl.ds(0, width)]), (hacc_hbm, hacc), (tacc_hbm, tacc))
        copies = [pltpu.make_async_copy(src, dst, sem.at[i]) for i, (src, dst) in enumerate(pairs)]
        for copy in copies:
            copy.start()
        copies[0].wait()
        rels = [rel_copies(rel_ids, rel_ref, rel_buf, rel_sem, k, tasks) for k in range(rounds)]
        for group in rels:
            for copy in group:
                copy.start()
        for copy in copies[1:4]:
            copy.wait()
        for k in range(rounds):
            for s in range(tasks):
                lanes[k * tasks + s] = jnp.full(lanes.shape[1:], lax.rem(rel_ids[k, 0, s], LANES), I32)
                gain[k * tasks + s] = jnp.full(gain.shape[1:], jnp.where(s < counts[0, k], HALF_NEG, 0.0), F32)
        make_labels(labels_ref, he, te, gain, 0, 0, tasks)
        for copy in rels[0] + copies[4:]:
            copy.wait()
        tail_out[pl.ds(width, 8), :] = jnp.broadcast_to(tacc[...], (8, LANES))
        scale_heads(head[...], lanes, rel_buf, 0, shi, slo, rel_out, tasks)
        for group in rels[1:]:
            for copy in group:
                copy.wait()

    return body


def tail_kernel(mine, k, tasks, width):
    def body(tail_in, shi, slo, labels_ref, gain, *refs):
        outs = refs[4:]

        @pl.when(role() == mine)
        def _():
            tail, state = tail_in[pl.ds(0, width), :], tail_in[pl.ds(width, 1), :]
            tail_step(tail, state, shi, slo, labels_ref, k * tasks, gain, k * tasks, outs[1:5], outs[0], tasks)

    return body


LABEL_ROUNDS = {(0, ODD): (1,), (1, ODD): (2, 3), (1, EVEN): (1, 2), (3, EVEN): (3,)}


def head_kernel(mine, m, tasks):
    done = m if mine == ODD else m - 1

    def body(he, te, rel_buf, lanes, gain, thi, tlo, chi, clo, *refs):
        ins, (head_out, hacc_out, shi, slo, rel_out, labels_ref) = refs[:5], refs[-6:]
        head, hacc, rel_in = ins[0], ins[1], ins[4]

        @pl.when(role() == mine)
        def _():
            new, state = head_step(head[...], hacc[...], (thi, tlo, chi, clo), rel_in, tasks)
            head_out[...] = new
            hacc_out[...] = state
            scale_heads(new, lanes, rel_buf, done + 1, shi, slo, rel_out, tasks)
            for k in LABEL_ROUNDS.get((m, mine), ()):
                make_labels(labels_ref, he, te, gain, k * tasks, k * tasks, tasks)

    return body


def last_heads(tasks):
    def body(head, hacc, rel_in, thi, tlo, chi, clo, head_out, hacc_out):
        head_out[...], hacc_out[...] = head_step(head[...], hacc[...], (thi, tlo, chi, clo), rel_in, tasks)

    return body


def pick_tails(mine, width):
    def body(packed, *refs):
        tail_out, tacc_out, row, sem = refs[-4:]

        @pl.when(role() == mine)
        def _():
            row[...] = packed[pl.ds(width, 1), :]
            copies = [pltpu.make_async_copy(packed.at[pl.ds(0, width)], tail_out, sem.at[0]), pltpu.make_async_copy(row, tacc_out, sem.at[1])]
            for copy in copies:
                copy.start()
            for copy in copies:
                copy.wait()

    return body


def call(body, ins, outs, scratch, args, alias=None):
    args = [pltpu.with_memory_space_constraint(a, pltpu.HBM) if spec is HBM else a for spec, a in zip(ins, args)]
    return pl.pallas_call(
        body,
        in_specs=ins,
        out_specs=[VMEM] * len(outs),
        out_shape=[jax.ShapeDtypeStruct(*o) for o in outs],
        scratch_shapes=scratch,
        input_output_aliases=alias or {},
        compiler_params=pltpu.CompilerParams(vmem_limit_bytes=16 << 20),
        cost_estimate=pl.CostEstimate(flops=10**9, bytes_accessed=1 << 20, transcendentals=0),
    )(*args)


def send_or_swap(block, distance, mine):
    n = lax.axis_size("blk")
    return lax.ppermute(block, "blk", [(i, (i + distance) % n if i % 2 == mine else i ^ 1) for i in range(n)])


def on_device(heads, tails, head_acc, tail_acc, relations, counts, rel_ids, head_edges, tail_edges):
    rounds, _, tasks, edges = head_edges.shape
    rows, width = heads.shape
    head, tail, rels = heads.T, tails.T, relations.T
    hacc, tacc, counts = head_acc.reshape(1, rows), tail_acc.reshape(1, rows), counts.T
    slots, groups, wide = rounds * tasks, edges // LANES, tasks * rows
    he, te = head_edges.reshape(slots, groups, LANES), tail_edges.reshape(slots, groups, LANES)
    block, packed, row = ((width, rows), F32), ((width + 8, rows), F32), ((1, rows), F32)
    coeff, scaled, half = ((rows, wide), BF16), ((width, wide), BF16), ((width, rows), BF16)
    table = ((slots, rows, rows), F32)
    kept_shapes = [half, half, coeff, coeff]
    state_shapes = [block, row, scaled, scaled, scaled, table]
    edge = ((slots, groups, LANES), I32)
    fixed_shapes = [edge, edge, ((slots, width, LANES), BF16), ((slots, 8, rows), I32), ((slots, 8, rows), F32)]

    def tails_step(mine, k, tail_in, kept, state):
        out = call(
            tail_kernel(mine, k, tasks, width), [VMEM] * 9, [packed] + kept_shapes, [],
            [tail_in, state[2], state[3], state[5], fixed[4]] + kept, {5 + i: 1 + i for i in range(4)})
        return out[0], list(out[1:])

    def heads_step(mine, m, kept, state):
        return list(call(
            head_kernel(mine, m, tasks), [VMEM] * 15, state_shapes, [],
            list(fixed) + kept + state, {9 + i: i for i in range(6)}))

    out = call(
        first_kernel(tasks, rounds, width), [HBM] * 9, [packed] + kept_shapes + state_shapes + fixed_shapes,
        [pltpu.SMEM(counts.shape, I32), pltpu.SMEM(rel_ids.shape, I32), pltpu.VMEM(*row),
         pltpu.SemaphoreType.DMA((slots,)), pltpu.SemaphoreType.DMA((8,))],
        [counts, rel_ids, head, tail, hacc, tacc, rels, he, te])
    start, kept, state, fixed = out[0], list(out[1:5]), list(out[5:11]), list(out[11:])
    own, kept = tails_step(ODD, 0, start, kept, state)
    to_even = send_or_swap(own, 1, ODD)
    own, kept = tails_step(EVEN, 0, start, kept, state)
    to_odd = send_or_swap(own, 1, EVEN)
    state = heads_step(ODD, 0, kept, state)
    for k in range(1, rounds):
        distance = 1 if k < rounds - 1 else 1 - rounds
        own, kept = tails_step(ODD, k, to_odd, kept, state)
        arrived = to_even
        to_even = send_or_swap(own, distance, ODD)
        if k < rounds - 1:
            state = heads_step(ODD, k, kept, state)
        state = heads_step(EVEN, k, kept, state)
        own, kept = tails_step(EVEN, k, arrived, kept, state)
        to_odd = send_or_swap(own, distance, EVEN)
    head, hacc = call(last_heads(tasks), [VMEM] * 7, [block, row], [], [state[0], state[1], state[4]] + kept)
    results = []
    for mine, packed_in in ((EVEN, to_even), (ODD, to_odd)):
        results = pl.pallas_call(
            pick_tails(mine, width),
            in_specs=[VMEM] + [HBM] * len(results),
            out_specs=[HBM] * 2,
            out_shape=[pltpu.HBM(*block), pltpu.HBM(*row)],
            scratch_shapes=[pltpu.VMEM(*row), pltpu.SemaphoreType.DMA((2,))],
            input_output_aliases={1 + i: i for i in range(len(results))},
            compiler_params=pltpu.CompilerParams(vmem_limit_bytes=16 << 20),
        )(packed_in, *results)
    tail, tacc = results
    return head.T, tail.T, hacc.reshape(rows), tacc.reshape(rows)


def solution(mesh):
    split, edge = P(("blk", "help"), None), P(None, ("blk", "help"), None, None)
    flat = P(("blk", "help"))

    return jax.shard_map(
        on_device,
        mesh=mesh,
        in_specs=(split, split, flat, flat, P(), P(None, ("blk", "help")), P(None, ("blk", "help"), None), edge, edge),
        out_specs=(split, split, flat, flat),
        check_vma=False,
    )
```

```python
import jax
import jax.numpy as jnp
from jax import lax
from jax.experimental import pallas as pl
from jax.experimental.pallas import tpu as pltpu
from jax.sharding import PartitionSpec as P


HALF_NEG = 0.0625 / 2
LEARN_RATE = 0.1
F32, BF16, I32 = jnp.float32, jnp.bfloat16, jnp.int32
LANES = 128
TAIL_GROUPS = ((0, 1), (1, 5))
ODD, EVEN = 1, 0
VMEM = pl.BlockSpec(memory_space=pltpu.VMEM)
SMEM = pl.BlockSpec(memory_space=pltpu.SMEM)
HBM = pl.BlockSpec(memory_space=pltpu.HBM)
NN, NT, TN = ((1,), (0,)), ((1,), (1,)), ((0,), (0,))


def role():
    return lax.rem(lax.axis_index("blk"), 2)


def dot(a, b, dims):
    return lax.dot_general(a, b, (dims, ((), ())), preferred_element_type=F32)


def hi_lo(x):
    hi = x.astype(BF16)
    return hi, (x - hi.astype(F32)).astype(BF16)


def cols(s):
    return pl.ds(s * LANES, LANES)


def one_hot(rows):
    which = lax.broadcasted_iota(I32, (LANES, LANES), 0).astype(F32).astype(BF16)
    one, zero = jnp.ones((), BF16), jnp.zeros((), BF16)
    parts = []
    for r in range(rows.shape[0]):
        row = jnp.broadcast_to(rows[r : r + 1, :].astype(F32), (16, LANES)).astype(BF16)
        parts.append(jnp.where(which == jnp.concatenate([row] * (LANES // 16), axis=0), one, zero))
    return jnp.concatenate(parts, axis=1)


def make_labels(labels_ref, he, te, gain, source, target, tasks):
    for s in range(tasks):
        count = dot(one_hot(te[source + s]), one_hot(he[source + s]), NT)
        labels_ref[target + s] = gain[source + s, 0:1, :] * (1.0 - count * (1.0 / HALF_NEG))


def rel_copies(rel_ids, rel_ref, rel_buf, sem, k, tasks):
    copies = []
    for s in range(tasks):
        start = pl.multiple_of((rel_ids[k, 0, s] // LANES) * LANES, LANES)
        copies.append(pltpu.make_async_copy(rel_ref.at[:, pl.ds(start, LANES)], rel_buf.at[k * tasks + s], sem.at[k * tasks + s]))
    return copies


def scale_heads(head, lanes, rel_buf, k, shi, slo, rel_out, tasks):
    which = lax.broadcasted_iota(I32, (LANES, LANES), 0)
    for first in range(0, tasks, 2):
        group = range(first, min(first + 2, tasks))
        picks = [(which == lanes[k * tasks + s, 0:1, :]).astype(F32).astype(BF16) for s in group]
        if len(group) == 2:
            none = jnp.zeros_like(picks[0])
            pick = jnp.concatenate([jnp.concatenate([picks[0], none], axis=1), jnp.concatenate([none, picks[1]], axis=1)], axis=0)
        else:
            pick = picks[0]
        rel = dot(jnp.concatenate([rel_buf[k * tasks + s] for s in group], axis=1), pick, NN)
        for i, s in enumerate(group):
            part = rel[:, i * LANES : (i + 1) * LANES]
            rel_out[:, cols(s)] = part.astype(BF16)
            shi[:, cols(s)], slo[:, cols(s)] = hi_lo(head * part)


def adagrad(block, state, grad):
    width = block.shape[0]
    square, part = grad * grad, width // 5
    square = (square[:part] + square[part : 2 * part]) + (square[2 * part : 3 * part] + square[3 * part : 4 * part]) + square[4 * part :]
    state = state + jnp.sum(square, axis=0, keepdims=True) * (1.0 / width)
    return block - grad * (LEARN_RATE * lax.rsqrt(state)), state


def tail_step(tail, state, shi_ref, slo_ref, labels_ref, label_row, gain_ref, gain_row, kept, tail_out, tasks):
    thi_ref, tlo_ref, chi_ref, clo_ref = kept
    width = tail.shape[0]
    thi, tlo = hi_lo(tail)
    thi_ref[...], tlo_ref[...] = thi, tlo
    shi, slo = shi_ref[...], slo_ref[...]
    both = dot(jnp.concatenate([thi, tlo], axis=1), shi, TN)
    scores = both[:LANES] + both[LANES:] + dot(thi, slo, TN)
    grad = None
    for first, stop in TAIL_GROUPS:
        stop = min(stop, tasks)
        parts = []
        for s in range(first, stop):
            score = scores[:, s * LANES : (s + 1) * LANES]
            parts.append(hi_lo(gain_ref[gain_row + s, 0:1, :] * jnp.tanh(0.5 * score) + labels_ref[label_row + s]))
        span = pl.ds(first * LANES, (stop - first) * LANES)
        chi, clo = (jnp.concatenate(part, axis=1) if len(part) > 1 else part[0] for part in zip(*parts))
        chi_ref[:, span], clo_ref[:, span] = chi, clo
        both = dot(shi_ref[:, span], jnp.concatenate([chi, clo], axis=0), NT)
        term = both[:, :LANES] + both[:, LANES:] + dot(slo_ref[:, span], chi, NT)
        grad = term if grad is None else grad + term
    tail, state = adagrad(tail, state, grad)
    tail_out[pl.ds(0, width), :] = tail
    tail_out[pl.ds(width, 8), :] = jnp.broadcast_to(state, (8, LANES))


def head_step(head, state, kept, rel_ref, tasks):
    thi_ref, tlo_ref, chi_ref, clo_ref = kept
    thi, tlo, chi = thi_ref[...], tlo_ref[...], chi_ref[...]
    wide = dot(jnp.concatenate([thi, tlo], axis=1), jnp.concatenate([chi, chi], axis=0), NN) + dot(thi, clo_ref[...], NN)
    grad = None
    for s in range(tasks):
        term = wide[:, s * LANES : (s + 1) * LANES] * rel_ref[:, cols(s)].astype(F32)
        grad = term if grad is None else grad + term
    return adagrad(head, state, grad)


def first_kernel(tasks, rounds, width):
    def body(counts_hbm, ids_hbm, head_hbm, tail_hbm, hacc_hbm, tacc_hbm, rel_ref, he_hbm, te_hbm, *refs):
        outs, (counts, rel_ids, tacc, rel_sem, sem) = refs[:16], refs[16:]
        tail_out, (head, hacc, shi, slo, rel_out, labels_ref), (he, te, rel_buf, lanes, gain) = outs[0], outs[5:11], outs[11:]
        pairs = ((ids_hbm, rel_ids), (counts_hbm, counts), (he_hbm, he), (te_hbm, te), (head_hbm, head),
                 (tail_hbm, tail_out.at[pl.ds(0, width)]), (hacc_hbm, hacc), (tacc_hbm, tacc))
        copies = [pltpu.make_async_copy(src, dst, sem.at[i]) for i, (src, dst) in enumerate(pairs)]
        for copy in copies:
            copy.start()
        copies[0].wait()
        rels = [rel_copies(rel_ids, rel_ref, rel_buf, rel_sem, k, tasks) for k in range(rounds)]
        for group in rels:
            for copy in group:
                copy.start()
        for copy in copies[1:4]:
            copy.wait()
        for k in range(rounds):
            for s in range(tasks):
                lanes[k * tasks + s] = jnp.full(lanes.shape[1:], lax.rem(rel_ids[k, 0, s], LANES), I32)
                gain[k * tasks + s] = jnp.full(gain.shape[1:], jnp.where(s < counts[0, k], HALF_NEG, 0.0), F32)
        make_labels(labels_ref, he, te, gain, 0, 0, tasks)
        for copy in rels[0] + copies[4:]:
            copy.wait()
        tail_out[pl.ds(width, 8), :] = jnp.broadcast_to(tacc[...], (8, LANES))
        scale_heads(head[...], lanes, rel_buf, 0, shi, slo, rel_out, tasks)
        for group in rels[1:]:
            for copy in group:
                copy.wait()

    return body


def tail_kernel(mine, k, tasks, width):
    def body(tail_in, shi, slo, labels_ref, gain, *refs):
        outs = refs[4:]

        @pl.when(role() == mine)
        def _():
            tail, state = tail_in[pl.ds(0, width), :], tail_in[pl.ds(width, 1), :]
            tail_step(tail, state, shi, slo, labels_ref, k * tasks, gain, k * tasks, outs[1:5], outs[0], tasks)

    return body


LABEL_ROUNDS = {(0, ODD): (1,), (1, ODD): (2, 3), (1, EVEN): (1, 2), (3, EVEN): (3,)}


def head_kernel(mine, m, tasks):
    done = m if mine == ODD else m - 1

    def body(he, te, rel_buf, lanes, gain, thi, tlo, chi, clo, *refs):
        ins, (head_out, hacc_out, shi, slo, rel_out, labels_ref) = refs[:5], refs[-6:]
        head, hacc, rel_in = ins[0], ins[1], ins[4]

        @pl.when(role() == mine)
        def _():
            new, state = head_step(head[...], hacc[...], (thi, tlo, chi, clo), rel_in, tasks)
            head_out[...] = new
            hacc_out[...] = state
            scale_heads(new, lanes, rel_buf, done + 1, shi, slo, rel_out, tasks)
            for k in LABEL_ROUNDS.get((m, mine), ()):
                make_labels(labels_ref, he, te, gain, k * tasks, k * tasks, tasks)

    return body


def last_heads(tasks):
    def body(head, hacc, rel_in, thi, tlo, chi, clo, head_out, hacc_out):
        head_out[...], hacc_out[...] = head_step(head[...], hacc[...], (thi, tlo, chi, clo), rel_in, tasks)

    return body


def pick_tails(mine, width):
    def body(packed, *refs):
        tail_out, tacc_out, row, sem = refs[-4:]

        @pl.when(role() == mine)
        def _():
            row[...] = packed[pl.ds(width, 1), :]
            part = width // 5
            copies = [pltpu.make_async_copy(row, tacc_out, sem.at[5])]
            for i in range(5):
                rows = pl.ds(i * part, part)
                copies.append(pltpu.make_async_copy(packed.at[rows], tail_out.at[rows], sem.at[i]))
            for copy in copies:
                copy.start()
            for copy in copies:
                copy.wait()

    return body


def call(body, ins, outs, scratch, args, alias=None):
    args = [pltpu.with_memory_space_constraint(a, pltpu.HBM) if spec is HBM else a for spec, a in zip(ins, args)]
    return pl.pallas_call(
        body,
        in_specs=ins,
        out_specs=[VMEM] * len(outs),
        out_shape=[jax.ShapeDtypeStruct(*o) for o in outs],
        scratch_shapes=scratch,
        input_output_aliases=alias or {},
        compiler_params=pltpu.CompilerParams(vmem_limit_bytes=16 << 20),
        cost_estimate=pl.CostEstimate(flops=10**9, bytes_accessed=1 << 20, transcendentals=0),
    )(*args)


def send_or_swap(block, distance, mine):
    n = lax.axis_size("blk")
    return lax.ppermute(block, "blk", [(i, (i + distance) % n if i % 2 == mine else i ^ 1) for i in range(n)])


def on_device(heads, tails, head_acc, tail_acc, relations, counts, rel_ids, head_edges, tail_edges):
    rounds, _, tasks, edges = head_edges.shape
    rows, width = heads.shape
    head, tail, rels = heads.T, tails.T, relations.T
    hacc, tacc, counts = head_acc.reshape(1, rows), tail_acc.reshape(1, rows), counts.T
    slots, groups, wide = rounds * tasks, edges // LANES, tasks * rows
    he, te = head_edges.reshape(slots, groups, LANES), tail_edges.reshape(slots, groups, LANES)
    block, packed, row = ((width, rows), F32), ((width + 8, rows), F32), ((1, rows), F32)
    coeff, scaled, half = ((rows, wide), BF16), ((width, wide), BF16), ((width, rows), BF16)
    table = ((slots, rows, rows), F32)
    kept_shapes = [half, half, coeff, coeff]
    state_shapes = [block, row, scaled, scaled, scaled, table]
    edge = ((slots, groups, LANES), I32)
    fixed_shapes = [edge, edge, ((slots, width, LANES), BF16), ((slots, 8, rows), I32), ((slots, 8, rows), F32)]

    def tails_step(mine, k, tail_in, kept, state):
        out = call(
            tail_kernel(mine, k, tasks, width), [VMEM] * 9, [packed] + kept_shapes, [],
            [tail_in, state[2], state[3], state[5], fixed[4]] + kept, {5 + i: 1 + i for i in range(4)})
        return out[0], list(out[1:])

    def heads_step(mine, m, kept, state):
        return list(call(
            head_kernel(mine, m, tasks), [VMEM] * 15, state_shapes, [],
            list(fixed) + kept + state, {9 + i: i for i in range(6)}))

    out = call(
        first_kernel(tasks, rounds, width), [HBM] * 9, [packed] + kept_shapes + state_shapes + fixed_shapes,
        [pltpu.SMEM(counts.shape, I32), pltpu.SMEM(rel_ids.shape, I32), pltpu.VMEM(*row),
         pltpu.SemaphoreType.DMA((slots,)), pltpu.SemaphoreType.DMA((8,))],
        [counts, rel_ids, head, tail, hacc, tacc, rels, he, te])
    start, kept, state, fixed = out[0], list(out[1:5]), list(out[5:11]), list(out[11:])
    own, kept = tails_step(ODD, 0, start, kept, state)
    to_even = send_or_swap(own, 1, ODD)
    own, kept = tails_step(EVEN, 0, start, kept, state)
    to_odd = send_or_swap(own, 1, EVEN)
    state = heads_step(ODD, 0, kept, state)
    for k in range(1, rounds):
        distance = 1 if k < rounds - 1 else 1 - rounds
        own, kept = tails_step(ODD, k, to_odd, kept, state)
        arrived = to_even
        to_even = send_or_swap(own, distance, ODD)
        if k < rounds - 1:
            state = heads_step(ODD, k, kept, state)
        state = heads_step(EVEN, k, kept, state)
        own, kept = tails_step(EVEN, k, arrived, kept, state)
        to_odd = send_or_swap(own, distance, EVEN)
    head, hacc = call(last_heads(tasks), [VMEM] * 7, [block, row], [], [state[0], state[1], state[4]] + kept)
    results = []
    for mine, packed_in in ((EVEN, to_even), (ODD, to_odd)):
        results = pl.pallas_call(
            pick_tails(mine, width),
            in_specs=[VMEM] + [HBM] * len(results),
            out_specs=[HBM] * 2,
            out_shape=[pltpu.HBM(*block), pltpu.HBM(*row)],
            scratch_shapes=[pltpu.VMEM(*row), pltpu.SemaphoreType.DMA((6,))],
            input_output_aliases={1 + i: i for i in range(len(results))},
            compiler_params=pltpu.CompilerParams(vmem_limit_bytes=16 << 20),
        )(packed_in, *results)
    tail, tacc = results
    return head.T, tail.T, hacc.reshape(rows), tacc.reshape(rows)


def solution(mesh):
    split, edge = P(("blk", "help"), None), P(None, ("blk", "help"), None, None)
    flat = P(("blk", "help"))

    return jax.shard_map(
        on_device,
        mesh=mesh,
        in_specs=(split, split, flat, flat, P(), P(None, ("blk", "help")), P(None, ("blk", "help"), None), edge, edge),
        out_specs=(split, split, flat, flat),
        check_vma=False,
    )
```
